128 devices in a mesh: row: 8 (over x, core), col: 16 (over y, z).
Axes of the slice: x: 4, y: 4, z: 4, core: 2. Of those that a mesh axis runs over, the one named last changes fastest.
Arguments:
- samples: float32 [384, 32768], P(None, ('row', 'col')), may hold values from -6 to 6
- omega_tiles: float32 [8, 16, 15, 256, 256], P('row', 'col'), may hold values from -6 to 6
- omega_diag: float32 [32768, 256], P(('row', 'col')), as said below
- tile_rows: int32 [8, 16, 15], P('row', 'col'), may hold values from 0 to 15, as said below
- tile_cols: int32 [8, 16, 15], P('row', 'col'), may hold values from 0 to 7
- tile_active: int32 [8, 16, 15], P('row', 'col'), may hold values from 0 to 1, as said below
Outputs:
- new_tiles: float32 [8, 16, 15, 256, 256], P('row', 'col')
- new_diag: float32 [32768, 256], P(('row', 'col'))
The draws below stay inside these ranges and needn't reach their ends.
Inputs may be any that keep to these rules, and one draw needn't show every extreme that they name: `tile_rows`: on each device the 15 listed tiles (I, J) are distinct and none is diagonal; with o = (J - I) mod (128), o is odd and below 64, or even and above it, so no tile is listed together with its mirror. `tile_active`: on each device the live slots come first and number at least 5; on device (0, 0) all are live. `omega_diag`: every diagonal tile is symmetric and its diagonal entries lie between 0.5 and 4.
All inputs are finite; a program needn't handle non-finite values.
Results may differ from the reference program's by a relative error of at most 0.0003.
Values sent between devices are 32-bit elements; how exact they have to be, the bound alone decides.
A program may use at most 128 MiB of HBM per device.

```python
import jax
import jax.numpy as jnp
from jax import lax

B = 256
NSAMP = 384
SLOTS = 15
P_SIZE = 32768
N_ROW = 8
N_COL = 16


def support_pair(key):
    device_count = N_ROW * N_COL
    half_count = device_count // 2
    offsets_all = jnp.arange(1, device_count, dtype=jnp.int32)
    odd_flag = offsets_all % 2
    valid = (odd_flag == 1) & (offsets_all < half_count) | (odd_flag == 0) & (offsets_all > half_count)

    def per_device(device):
        row_index = device // N_COL
        col_index = device % N_COL
        ranks = jax.random.permutation(jax.random.fold_in(key, device), device_count - 1).astype(jnp.int32)
        scores = jnp.where(valid, ranks, ranks + device_count)
        order = jnp.argsort(scores, stable=True).astype(jnp.int32)
        offsets = offsets_all[order[:SLOTS]]
        block_row = (col_index - offsets) % N_COL
        steps_up = (offsets - (col_index - block_row)) % device_count // N_COL
        block_col = (row_index + steps_up) % N_ROW
        return (block_row.astype(jnp.int32), block_col.astype(jnp.int32))
    rows_all, cols_all = jax.vmap(per_device)(jnp.arange(device_count, dtype=jnp.int32))
    return (rows_all.reshape(N_ROW, N_COL, SLOTS), cols_all.reshape(N_ROW, N_COL, SLOTS))


def draw_tile_rows(key, part):
    return support_pair(jax.random.fold_in(key, 11))[0]


def draw_tile_cols(key, part):
    return support_pair(jax.random.fold_in(key, 11))[1]


def draw_tile_active(key, part):
    device_count = N_ROW * N_COL
    live_count = jax.random.randint(jax.random.fold_in(key, 23), (device_count,), SLOTS // 3, SLOTS + 1)
    live_count = live_count.at[0].set(SLOTS)
    slots_iota = jnp.arange(SLOTS, dtype=jnp.int32)
    mask_all = (slots_iota[None, :] < live_count[:, None]).astype(jnp.int32)
    return mask_all.reshape(N_ROW, N_COL, SLOTS)


def draw_omega_diag(key, part):
    block_count = N_ROW * N_COL
    first_key = jax.random.fold_in(key, 31)
    second_key = jax.random.fold_in(key, 37)
    off_part = jax.random.normal(first_key, (block_count, B, B), jnp.float32)
    logs = jax.random.uniform(second_key, (block_count, B), jnp.float32, jnp.log(0.6), jnp.log(3.5))
    off_part = (off_part + jnp.transpose(off_part, (0, 2, 1))) * 0.70710678
    identity = jnp.eye(B, dtype=jnp.float32)
    tiles_all = off_part * (1.0 - identity[None]) + identity[None] * jnp.exp(logs)[:, None, :]
    return tiles_all.reshape(block_count * B, B).astype(jnp.float32)


def shard_levels(rng, shape, pieces, smallest, largest):
    loudness = 1.0
    for axis_at, shards_of in pieces:
        heights = jax.random.uniform(jax.random.fold_in(jax.random.fold_in(rng, 6), axis_at), (shards_of,), jnp.float32, smallest / len(pieces), largest / len(pieces))
        loudness = loudness * jnp.repeat(jnp.exp(heights), shape[axis_at] // shards_of).reshape((-1,) + (1,) * (len(shape) - 1 - axis_at))
    return loudness


def normal_values(stream_key, shape, spread, most, split=(), kind=jnp.bfloat16):
    array = jax.random.normal(stream_key, shape, jnp.float32) * spread
    if len(split) > 0:
        array = shard_levels(stream_key, shape, split, -0.22, 0.18) * array
    return jnp.clip(array, min=-most, max=most).astype(kind)


def setup_inputs(seed: int = 0) -> dict:
    key_of = jax.random.split(jax.random.key(seed), 7)
    samples = normal_values(key_of[0], (NSAMP, P_SIZE), 1.0, 6.0, ((1, 128),), jnp.float32)
    omega_tiles = normal_values(key_of[1], (N_ROW, N_COL, SLOTS, B, B), 1.0, 6.0, ((0, 8), (1, 16)), jnp.float32)
    omega_diag = draw_omega_diag(jax.random.fold_in(key_of[6], 71), 0)
    tile_rows = draw_tile_rows(jax.random.fold_in(key_of[6], 71), 0)
    tile_cols = draw_tile_cols(jax.random.fold_in(key_of[6], 71), 0)
    tile_active = draw_tile_active(jax.random.fold_in(key_of[6], 71), 0)
    return dict(samples=samples, omega_tiles=omega_tiles, omega_diag=omega_diag, tile_rows=tile_rows, tile_cols=tile_cols, tile_active=tile_active)


HIGHEST = lax.Precision.HIGHEST
STEP_SIZE = 0.05
PENALTY = 4.0


def soft_shrink(values, limit):
    return jnp.sign(values) * jnp.maximum(jnp.abs(values) - limit, 0.0)


def reference(samples, omega_tiles, omega_diag, tile_rows, tile_cols, tile_active):
    block_count = N_ROW * N_COL
    blocks = jnp.transpose(samples.reshape(NSAMP, block_count, B), (1, 0, 2))
    devices = jnp.arange(block_count, dtype=jnp.int32)
    global_rows = ((devices // N_COL)[:, None] * N_COL + tile_rows.reshape(block_count, SLOTS)).astype(jnp.int32)
    global_cols = (tile_cols.reshape(block_count, SLOTS) * N_COL + (devices % N_COL)[:, None]).astype(jnp.int32)
    active_all = tile_active.reshape(block_count, SLOTS)
    tile_set = omega_tiles.reshape(block_count, SLOTS, B, B)
    diag_tiles = omega_diag.reshape(block_count, B, B)
    z_start = jnp.einsum('dnk,dkl->dnl', blocks, diag_tiles, precision=HIGHEST)

    def accumulate(z_total, element):
        tiles_here, rows_here, cols_here = element
        z_total = z_total.at[cols_here].add(jnp.einsum('snk,skl->snl', blocks[rows_here], tiles_here, precision=HIGHEST))
        z_total = z_total.at[rows_here].add(jnp.einsum('snl,skl->snk', blocks[cols_here], tiles_here, precision=HIGHEST))
        return z_total, None

    z_full, _ = lax.scan(accumulate, z_start, (tile_set, global_rows, global_cols))

    def update(state, element):
        tiles_here, rows_here, cols_here, active_here = element
        gradient = jnp.einsum('snk,snl->skl', blocks[rows_here], z_full[cols_here], precision=HIGHEST)
        gradient = gradient + jnp.einsum('snk,snl->skl', z_full[rows_here], blocks[cols_here], precision=HIGHEST)
        gradient = gradient / (2.0 * NSAMP)
        stepped = tiles_here - STEP_SIZE * gradient
        updated = jnp.where(active_here[:, None, None] > 0, soft_shrink(stepped, STEP_SIZE * PENALTY), tiles_here)
        return state, updated

    _, new_tiles = lax.scan(update, jnp.zeros((), jnp.float32), (tile_set, global_rows, global_cols, active_all))
    inverse = 1.0 / jnp.diagonal(diag_tiles, axis1=1, axis2=2)
    identity = jnp.eye(B, dtype=jnp.float32)
    diag_grad = jnp.einsum('dnk,dnl->dkl', blocks, z_full, precision=HIGHEST)
    diag_grad = diag_grad + jnp.einsum('dnk,dnl->dkl', z_full, blocks, precision=HIGHEST)
    diag_grad = diag_grad / (2.0 * NSAMP) - identity[None] * inverse[:, None, :]
    diag_step = diag_tiles - STEP_SIZE * diag_grad
    new_diag = jnp.where(identity[None] > 0, diag_step, soft_shrink(diag_step, STEP_SIZE * PENALTY))
    return new_tiles.reshape(N_ROW, N_COL, SLOTS, B, B), new_diag.reshape(P_SIZE, B)
```

```python
import functools

import jax
import jax.numpy as jnp
from jax import lax
from jax.experimental import pallas as pl
from jax.experimental.pallas import tpu as pltpu
from jax.sharding import PartitionSpec as P

MESH = pl.DeviceIdType.MESH
F32 = jnp.float32
BF16 = jnp.bfloat16
STEP_SIZE = 0.05
PENALTY = 4.0
SIDE = 4
NN = (((1,), (0,)), ((), ()))
NT = (((1,), (1,)), ((), ()))
TN = (((0,), (0,)), ((), ()))
ROUTES = ((True, 1), (True, -1), (False, 1), (False, -1))


def split(v):
    high = v.astype(BF16)
    low = (v - high.astype(F32)).astype(BF16)
    return high, low


def dot3(a, b, dims):
    ah, al = split(a)
    bh, bl = split(b)
    dot = functools.partial(lax.dot_general, dimension_numbers=dims, preferred_element_type=F32)
    return dot(ah, bh) + dot(ah, bl) + dot(al, bh)


def mod4(v):
    return lax.rem(v + 2 * SIDE, SIDE)


def shrink(v, limit):
    return jnp.where(v > 0, 1.0, -1.0) * jnp.maximum(jnp.abs(v) - limit, 0.0)


def kernel(
    xt, tiles_hbm, diag_ref, left, right, active, out_hbm, diag_out,
    xrow, xcol, zrow, zcol, tile, pw, py, rs0, rsb, rsa, ys, yx, yr, ids, lists,
    xa_s, xa_r, xb_s, xb_r, za_s, za_r, zb_s, zb_r, wa_s, wa_r, wb_s, wb_r,
    xh_s, xh_r, xp_s, xp_r, zh_s, zh_r, zp_s, zp_r, yh_s, yh_r, yp_s, yp_r,
    in_sem, out_sem,
):
    slots = left.shape[0]
    side, samp = xt.shape
    quarter, half = side // 4, side // 2
    r = lax.axis_index("row")
    c = lax.axis_index("col")
    x, core = lax.div(r, 2), lax.rem(r, 2)
    yy, zz = lax.div(c, SIDE), lax.rem(c, SIDE)
    other = 1 - core
    partner = 2 * x + other
    pos_a = [zz if first else yy for first, _ in ROUTES]
    pos_b = [yy if first else zz for first, _ in ROUTES]

    def col_of(q, a, b):
        return b * SIDE + a if ROUTES[q][0] else a * SIDE + b

    def qrows(q):
        return pl.ds(q * quarter, quarter)

    def hrows(g):
        return pl.ds(g * half, half)

    def remote(src, dst, send, recv, row, col):
        return pltpu.make_async_remote_copy(
            src_ref=src, dst_ref=dst, send_sem=send, recv_sem=recv,
            device_id=(row, col), device_id_type=MESH,
        )

    def next_a(q):
        return col_of(q, mod4(pos_a[q] + ROUTES[q][1]), pos_b[q])

    def next_b(q):
        return col_of(q, pos_a[q], mod4(pos_b[q] + ROUTES[q][1]))

    def next_x(g):
        return 2 * mod4(x + (1, -1)[g]) + core

    barrier = pltpu.get_barrier_semaphore()
    peers = [(r, next_a(q)) for q in range(4)]
    peers += [(next_x(0), c), (next_x(1), c), (partner, c)]
    for row, col in peers:
        pl.semaphore_signal(barrier, inc=1, device_id=(row, col), device_id_type=MESH)
    pl.semaphore_wait(barrier, len(peers))

    def gather_a(panel, q, h, own, sems):
        d = ROUTES[q][1]
        at = col_of(q, mod4(pos_a[q] - d * h), pos_b[q])
        src = own.at[qrows(q)] if h == 0 else panel.at[at, qrows(q)]
        return remote(src, panel.at[at, qrows(q)], sems[0].at[q, h], sems[1].at[q, h], r, next_a(q))

    def gather_a_arrival(panel, q, h, sems):
        d = ROUTES[q][1]
        at = col_of(q, mod4(pos_a[q] - d * (h + 1)), pos_b[q])
        ref = panel.at[at, qrows(q)]
        return remote(ref, ref, sems[0].at[q, h], sems[1].at[q, h], r, next_a(q))

    def gather_b(panel, q, i, own, sems):
        d = ROUTES[q][1]
        at = col_of(q, mod4(pos_a[q] - d * lax.rem(i, 4)), mod4(pos_b[q] - d * lax.div(i, 4)))
        src = panel.at[at, qrows(q)] if own is None else own.at[qrows(q)]
        return remote(src, panel.at[at, qrows(q)], sems[2].at[q, i], sems[3].at[q, i], r, next_b(q))

    def gather_b_arrival(panel, q, i, sems):
        d = ROUTES[q][1]
        at = col_of(q, mod4(pos_a[q] - d * lax.rem(i, 4)), mod4(pos_b[q] - d * (lax.div(i, 4) + 1)))
        ref = panel.at[at, qrows(q)]
        return remote(ref, ref, sems[2].at[q, i], sems[3].at[q, i], r, next_b(q))

    def ring(panel, g, h, own, sems):
        at = 2 * mod4(x - (1, -1)[g] * h) + core
        src = own.at[hrows(g)] if h == 0 else panel.at[at, hrows(g)]
        return remote(src, panel.at[at, hrows(g)], sems[0].at[g, h], sems[1].at[g, h], next_x(g), c)

    def ring_arrival(panel, g, h, sems):
        at = 2 * mod4(x - (1, -1)[g] * (h + 1)) + core
        ref = panel.at[at, hrows(g)]
        return remote(ref, ref, sems[0].at[g, h], sems[1].at[g, h], next_x(g), c)

    def hand(panel, g, h, own, sems):
        at = 2 * mod4(x - (1, -1)[g] * h) + core
        src = own.at[hrows(g)] if h == 0 else panel.at[at, hrows(g)]
        return remote(src, panel.at[at, hrows(g)], sems[2].at[g, h], sems[3].at[g, h], partner, c)

    def hand_arrival(panel, g, h, sems):
        at = 2 * mod4(x - (1, -1)[g] * h) + other
        ref = panel.at[at, hrows(g)]
        return remote(ref, ref, sems[2].at[g, h], sems[3].at[g, h], partner, c)

    def gather_phase(rowp, colp, own_row, own_col, csems, rsems, work, between, first_work):
        for q in range(4):
            gather_a(rowp, q, 0, own_row, csems).start()
        for g in range(2):
            ring(colp, g, 0, own_col, rsems).start()
            hand(colp, g, 0, own_col, rsems).start()
        for q in range(4):
            gather_b(rowp, q, 0, own_row, csems).start()
        first_work()

        def hop_a(h):
            for q in range(4):
                gather_a_arrival(rowp, q, h, csems).wait_recv()
                if h < 2:
                    gather_a(rowp, q, h + 1, own_row, csems).start()
                gather_b(rowp, q, h + 1, None, csems).start()

        def hop_x(h):
            for g in range(2):
                ring_arrival(colp, g, h, rsems).wait_recv()
                if h < 2:
                    ring(colp, g, h + 1, own_col, rsems).start()
                hand(colp, g, h + 1, own_col, rsems).start()

        def hop_b(i, forward):
            for q in range(4):
                gather_b_arrival(rowp, q, i, csems).wait_recv()
                if forward:
                    gather_b(rowp, q, i + 4, None, csems).start()

        hop_a(0)
        hop_a(1)
        hop_x(0)
        hop_a(2)
        hop_x(1)
        hop_b(0, True)
        hop_b(1, True)
        hop_x(2)
        hop_b(2, True)
        hop_b(3, True)
        for g in range(2):
            for h in range(4):
                hand_arrival(colp, g, h, rsems).wait_recv()

        @pl.loop(0, 4)
        def _(i):
            hop_b(i + 4, True)
            for k in range(4):
                work(i * 4 + k)

        between()

        @pl.loop(8, 12)
        def _(i):
            hop_b(i, False)

    def gather_drain(rowp, colp, own_row, own_col, csems, rsems):
        for q in range(4):
            for h in range(3):
                gather_a(rowp, q, h, own_row, csems).wait_send()

        @pl.loop(0, 12)
        def _(i):
            for q in range(4):
                gather_b(rowp, q, i, None, csems).wait_send()

        for g in range(2):
            for h in range(3):
                ring(colp, g, h, own_col, rsems).wait_send()
            for h in range(4):
                hand(colp, g, h, own_col, rsems).wait_send()

    def w_sum(col, rows):
        packed = lists[0, col]
        total = pw[packed & 15, rows, :]
        for j in range(1, 4):
            total = total + pw[lax.shift_right_arithmetic(packed, 4 * j) & 15, rows, :]
        return total

    def y_sum(row, rows):
        packed = lists[1, row]
        total = py[packed & 15, rows, :]
        for j in range(1, 8):
            total = total + py[lax.shift_right_arithmetic(packed, 4 * j) & 15, rows, :]
        return total

    def tile_in(s):
        return pltpu.make_async_copy(tiles_hbm.at[s], tile.at[s], in_sem.at[s])

    xsem = (xa_s, xa_r, xb_s, xb_r)
    zsem = (za_s, za_r, zb_s, zb_r)
    xrsem = (xh_s, xh_r, xp_s, xp_r)
    zrsem = (zh_s, zh_r, zp_s, zp_r)

    def start_work():
        for s in range(slots):
            tile_in(s).start()
        xrow[c] = xt[...]
        xcol[r] = xt[...]
        tile[slots] = diag_ref[...]
        pw[0] = jnp.zeros((side, samp), F32)
        py[0] = jnp.zeros((side, samp), F32)
        for s in range(slots):
            ids[0, s] = left[s]
            ids[1, s] = right[s]
            ids[2, s] = active[s]
        ids[0, slots] = c
        ids[1, slots] = r
        ids[2, slots] = 1

        def packs(which, n):
            @pl.loop(0, n)
            def _(a):
                packed = jnp.int32(0)
                for s in range(slots):
                    ident = left[s] if which == 0 else right[s]
                    packed = jnp.where(ident == a, packed * 16 + (s + 1), packed)
                lists[which, a] = packed

        packs(0, 16)
        packs(1, 8)
        for s in range(slots):
            tile_in(s).wait()

    def w_product(s):
        pw[s + 1] = dot3(tile[s], xcol[ids[1, s]], NN)

    def y_product(s):
        py[s + 1] = dot3(tile[s], xrow[ids[0, s]], TN)

    def scatter_target(q, h, j):
        d = ROUTES[q][1]
        return col_of(q, mod4(pos_a[q] - d * (j + 1)), mod4(pos_b[q] - d * (h + 1)))

    def scatter_b0(q, j):
        return remote(rs0.at[q, j], rsb.at[q, j], wb_s.at[q, j], wb_r.at[q, j], r, next_b(q))

    def scatter_b(q, i):
        return remote(rsb.at[q, i], rsb.at[q, i + 4], wb_s.at[q, i + 4], wb_r.at[q, i + 4], r, next_b(q))

    def scatter_b_arrival(q, i):
        return remote(rsb.at[q, i], rsb.at[q, i], wb_s.at[q, i], wb_r.at[q, i], r, next_b(q))

    def scatter_a(q, h):
        src = rsb.at[q, 8] if h == 0 else rsa.at[q, h - 1]
        return remote(src, rsa.at[q, h], wa_s.at[q, h], wa_r.at[q, h], r, next_a(q))

    def scatter_a_arrival(q, h):
        return remote(rsa.at[q, h], rsa.at[q, h], wa_s.at[q, h], wa_r.at[q, h], r, next_a(q))

    def scatter_start():
        for j in range(4):
            for q in range(4):
                rs0[q, j] = w_sum(scatter_target(q, 0, j), qrows(q))
            for q in range(4):
                scatter_b0(q, j).start()

    def scatter_hop(i, forward):
        h, j = lax.div(i, 4) + 1, lax.rem(i, 4)
        for q in range(4):
            scatter_b_arrival(q, i).wait_recv()
            rsb[q, i] = rsb[q, i] + w_sum(scatter_target(q, h, j), qrows(q))
            if forward:
                scatter_b(q, i).start()

    def y_target(g, h):
        return mod4(x - (1, -1)[g] * (h + 1))

    def y_give(g, h):
        return remote(ys.at[g, h], yx.at[g, h], yp_s.at[g, h], yp_r.at[g, h], partner, c)

    def y_ring(g, h):
        src = yx.at[g, 0] if h == 0 else yr.at[g, h - 1]
        return remote(src, yr.at[g, h], yh_s.at[g, h], yh_r.at[g, h], next_x(g), c)

    def y_exchange(h):
        for g in range(2):
            ys[g, h] = y_sum(2 * y_target(g, h) + other, hrows(g))
        for g in range(2):
            y_give(g, h).start()

    def y_combine(h):
        for g in range(2):
            y_give(g, h).wait_recv()
            yx[g, h] = yx[g, h] + y_sum(2 * y_target(g, h) + core, hrows(g))
        if h == 0:
            for g in range(2):
                y_ring(g, 0).start()

    def y_hop(h):
        for g in range(2):
            y_ring(g, h - 1).wait_recv()
            yr[g, h - 1] = yr[g, h - 1] + yx[g, h]
            if h < 3:
                y_ring(g, h).start()

    gather_phase(xrow, xcol, xt, xt, xsem, xrsem, w_product, scatter_start, start_work)

    @pl.loop(0, 4)
    def _(i):
        scatter_hop(i, True)
        for k in range(4):
            y_product(jnp.minimum(i * 4 + k, slots - 1))

    for h in range(4):
        y_exchange(h)
    scatter_hop(4, True)
    y_combine(0)
    scatter_hop(5, True)
    y_combine(1)
    scatter_hop(6, True)
    y_combine(2)
    y_combine(3)
    scatter_hop(7, True)
    y_hop(1)
    scatter_hop(8, False)
    for q in range(4):
        scatter_a(q, 0).start()
    scatter_hop(9, False)
    y_hop(2)
    for h in range(1, 3):
        if h == 2:
            scatter_hop(10, False)
        for q in range(4):
            scatter_a_arrival(q, h - 1).wait_recv()
            rsa[q, h - 1] = rsa[q, h - 1] + rsb[q, 8 + h]
            scatter_a(q, h).start()
    scatter_hop(11, False)
    y_hop(3)
    for q in range(4):
        scatter_a_arrival(q, 2).wait_recv()
        part = pl.ds((q % 2) * quarter, quarter)
        total = rsa[q, 2] + rsb[q, 11] + yr[q // 2, 2, part, :] + pw[slots + 1, qrows(q), :]
        zrow[c, qrows(q), :] = total
        zcol[r, qrows(q), :] = total

    scale = STEP_SIZE / (2.0 * samp)

    def first_half(s):
        factor = scale * ids[2, s].astype(F32)
        grad = dot3(xrow[ids[0, s]], zcol[ids[1, s]], NT)
        tile[s] = tile[s] - factor * grad

    gather_phase(
        zrow, zcol, zrow.at[c], zcol.at[r], zsem, zrsem, first_half, lambda: None, lambda: None
    )

    def tile_out(s):
        return pltpu.make_async_copy(tile.at[s], out_hbm.at[s], out_sem.at[s])

    def second_half(s):
        factor = scale * ids[2, s].astype(F32)
        grad = dot3(zrow[ids[0, s]], xcol[ids[1, s]], NT)
        return tile[s] - factor * grad

    @pl.loop(0, slots)
    def _(s):
        limit = STEP_SIZE * PENALTY * ids[2, s].astype(F32)
        tile[s] = shrink(second_half(s), limit)
        tile_out(s).start()

    stepped = second_half(slots)
    eye = lax.broadcasted_iota(jnp.int32, (side, side), 0) == lax.broadcasted_iota(
        jnp.int32, (side, side), 1
    )
    inverse = STEP_SIZE / jnp.where(eye, diag_ref[...], 1.0)
    diag_out[...] = jnp.where(eye, stepped + inverse, shrink(stepped, STEP_SIZE * PENALTY))

    gather_drain(xrow, xcol, xt, xt, xsem, xrsem)
    gather_drain(zrow, zcol, zrow.at[c], zcol.at[r], zsem, zrsem)
    for q in range(4):
        for j in range(4):
            scatter_b0(q, j).wait_send()
        for i in range(8):
            scatter_b(q, i).wait_send()
        for h in range(3):
            scatter_a(q, h).wait_send()
    for g in range(2):
        for h in range(4):
            y_give(g, h).wait_send()
        for h in range(3):
            y_ring(g, h).wait_send()
    for s in range(slots):
        tile_out(s).wait()


def per_device(samples, omega_tiles, omega_diag, tile_rows, tile_cols, tile_active):
    rows, cols = lax.axis_size("row"), lax.axis_size("col")
    samp, side = samples.shape
    slots = omega_tiles.shape[2]
    block = (side, samp)
    dma = pltpu.SemaphoreType.DMA
    vmem = pl.BlockSpec(memory_space=pltpu.VMEM)
    smem = pl.BlockSpec(memory_space=pltpu.SMEM)
    anyw = pl.BlockSpec(memory_space=pl.ANY)
    gather = [dma((4, 3)), dma((4, 3)), dma((4, 12)), dma((4, 12))]
    line = [dma((2, 3)), dma((2, 3)), dma((2, 4)), dma((2, 4))]
    new_tiles, new_diag = pl.pallas_call(
        kernel,
        out_shape=(
            jax.ShapeDtypeStruct((slots, side, side), F32),
            jax.ShapeDtypeStruct((side, side), F32),
        ),
        in_specs=[vmem, anyw, vmem, smem, smem, smem],
        out_specs=(anyw, vmem),
        scratch_shapes=[
            pltpu.VMEM((cols,) + block, F32),
            pltpu.VMEM((rows,) + block, F32),
            pltpu.VMEM((cols,) + block, F32),
            pltpu.VMEM((rows,) + block, F32),
            pltpu.VMEM((slots + 1, side, side), F32),
            pltpu.VMEM((slots + 2,) + block, F32),
            pltpu.VMEM((slots + 1,) + block, F32),
            pltpu.VMEM((4, 4, side // 4, samp), F32),
            pltpu.VMEM((4, 12, side // 4, samp), F32),
            pltpu.VMEM((4, 3, side // 4, samp), F32),
            pltpu.VMEM((2, 4, side // 2, samp), F32),
            pltpu.VMEM((2, 4, side // 2, samp), F32),
            pltpu.VMEM((2, 3, side // 2, samp), F32),
            pltpu.SMEM((3, slots + 1), jnp.int32),
            pltpu.SMEM((2, 16), jnp.int32),
        ]
        + gather + gather + gather + line + line + line
        + [dma((slots,)), dma((slots,))],
        compiler_params=pltpu.CompilerParams(
            collective_id=0, has_side_effects=True, vmem_limit_bytes=62 * 1024 * 1024
        ),
    )(
        samples.T,
        omega_tiles.reshape(slots, side, side),
        omega_diag,
        tile_rows.reshape(slots),
        tile_cols.reshape(slots),
        tile_active.reshape(slots),
    )
    return new_tiles[None, None], new_diag


def solution(mesh):
    in_specs = (
        P(None, ("row", "col")),
        P("row", "col", None, None, None),
        P(("row", "col"), None),
        P("row", "col", None),
        P("row", "col", None),
        P("row", "col", None),
    )
    out_specs = (P("row", "col", None, None, None), P(("row", "col"), None))
    return jax.shard_map(
        per_device, mesh=mesh, in_specs=in_specs, out_specs=out_specs, check_vma=False
    )
```

```python
import functools

import jax
import jax.numpy as jnp
from jax import lax
from jax.experimental import pallas as pl
from jax.experimental.pallas import tpu as pltpu
from jax.sharding import PartitionSpec as P

MESH = pl.DeviceIdType.MESH
F32 = jnp.float32
BF16 = jnp.bfloat16
STEP_SIZE = 0.05
PENALTY = 4.0
SIDE = 4
NN = (((1,), (0,)), ((), ()))
NT = (((1,), (1,)), ((), ()))
TN = (((0,), (0,)), ((), ()))
ROUTES = ((True, 1), (True, -1), (False, 1), (False, -1))


def split(v):
    high = v.astype(BF16)
    low = (v - high.astype(F32)).astype(BF16)
    return high, low


def dot3(a, b, dims):
    ah, al = split(a)
    bh, bl = split(b)
    dot = functools.partial(lax.dot_general, dimension_numbers=dims, preferred_element_type=F32)
    return dot(ah, bh) + dot(ah, bl) + dot(al, bh)


def mod4(v):
    return lax.rem(v + 2 * SIDE, SIDE)


def shrink(v, limit):
    return jnp.where(v > 0, 1.0, -1.0) * jnp.maximum(jnp.abs(v) - limit, 0.0)


def kernel(
    samples_hbm, tiles_hbm, diag_hbm, left, right, active,
    tile, zh, zl, xh, xl, ids,
    raw, xt, xrow, xcol, zrow, zcol, pw, py, rs0, rsb, rsa, ys, yx, yr, lists,
    ga_r, gb_r, xf_r, zf_r, gh_r, gp_r, wa_r, wb_r, yh_r, yp_r,
    x_s, xr_s, z_s, zr_s, w_s, y_s, in_sem,
):
    slots = left.shape[0]
    samp, side = raw.shape
    quarter, half = side // 4, side // 2
    r = lax.axis_index("row")
    c = lax.axis_index("col")
    x, core = lax.div(r, 2), lax.rem(r, 2)
    yy, zz = lax.div(c, SIDE), lax.rem(c, SIDE)
    other = 1 - core
    partner = 2 * x + other
    pos_a = [zz if first else yy for first, _ in ROUTES]
    pos_b = [yy if first else zz for first, _ in ROUTES]

    def col_of(q, a, b):
        return b * SIDE + a if ROUTES[q][0] else a * SIDE + b

    def qrows(q):
        return pl.ds(q * quarter, quarter)

    def hrows(g):
        return pl.ds(g * half, half)

    def remote(src, dst, send, recv, row, col):
        return pltpu.make_async_remote_copy(
            src_ref=src, dst_ref=dst, send_sem=send, recv_sem=recv,
            device_id=(row, col), device_id_type=MESH,
        )

    def next_a(q):
        return col_of(q, mod4(pos_a[q] + ROUTES[q][1]), pos_b[q])

    def next_b(q):
        return col_of(q, pos_a[q], mod4(pos_b[q] + ROUTES[q][1]))

    def next_x(g):
        return 2 * mod4(x + (1, -1)[g]) + core

    barrier = pltpu.get_barrier_semaphore()
    peers = [(r, next_a(q)) for q in range(4)]
    peers += [(next_x(0), c), (next_x(1), c), (partner, c)]
    for row, col in peers:
        pl.semaphore_signal(barrier, inc=1, device_id=(row, col), device_id_type=MESH)
    loads = [
        pltpu.make_async_copy(samples_hbm, raw, in_sem.at[0]),
        pltpu.make_async_copy(tiles_hbm, tile.at[pl.ds(0, slots)], in_sem.at[1]),
        pltpu.make_async_copy(diag_hbm, tile.at[slots], in_sem.at[2]),
    ]
    for load in loads:
        load.start()
    loads[0].wait()
    own = raw[...].T
    xt[...] = own
    xrow[c] = own
    xcol[r] = own
    pw[0] = jnp.zeros((side, samp), F32)
    py[0] = jnp.zeros((side, samp), F32)
    pl.semaphore_wait(barrier, len(peers))

    def gather_a(panel, q, h, own, sems):
        d = ROUTES[q][1]
        at = col_of(q, mod4(pos_a[q] - d * h), pos_b[q])
        src = own.at[qrows(q)] if h == 0 else panel.at[at, qrows(q)]
        return remote(src, panel.at[at, qrows(q)], sems[0], ga_r.at[q, h], r, next_a(q))

    def gather_a_arrival(panel, q, h, sems):
        d = ROUTES[q][1]
        at = col_of(q, mod4(pos_a[q] - d * (h + 1)), pos_b[q])
        ref = panel.at[at, qrows(q)]
        return remote(ref, ref, sems[0], ga_r.at[q, h], r, next_a(q))

    def gather_b(panel, q, i, own, sems, last=False):
        d = ROUTES[q][1]
        at = col_of(q, mod4(pos_a[q] - d * lax.rem(i, 4)), mod4(pos_b[q] - d * lax.div(i, 4)))
        src = panel.at[at, qrows(q)] if own is None else own.at[qrows(q)]
        recv = sems[1] if last else gb_r.at[q, i]
        return remote(src, panel.at[at, qrows(q)], sems[0], recv, r, next_b(q))

    def arrived_b(q, i):
        d = ROUTES[q][1]
        return col_of(q, mod4(pos_a[q] - d * lax.rem(i, 4)), mod4(pos_b[q] - d * (lax.div(i, 4) + 1)))

    def gather_b_arrival(panel, q, i, sems):
        ref = panel.at[arrived_b(q, i), qrows(q)]
        return remote(ref, ref, sems[0], gb_r.at[q, i], r, next_b(q))

    def gather_last(panel, sems):
        ref = panel.at[pl.ds(0, 4)]
        return remote(ref, ref, sems[0], sems[1], r, next_b(0))

    def ring(panel, g, h, own, sems):
        at = 2 * mod4(x - (1, -1)[g] * h) + core
        src = own.at[hrows(g)] if h == 0 else panel.at[at, hrows(g)]
        return remote(src, panel.at[at, hrows(g)], sems[0], gh_r.at[g, h], next_x(g), c)

    def ring_arrival(panel, g, h, sems):
        at = 2 * mod4(x - (1, -1)[g] * (h + 1)) + core
        ref = panel.at[at, hrows(g)]
        return remote(ref, ref, sems[0], gh_r.at[g, h], next_x(g), c)

    def hand(panel, g, h, own, sems):
        at = 2 * mod4(x - (1, -1)[g] * h) + core
        src = own.at[hrows(g)] if h == 0 else panel.at[at, hrows(g)]
        return remote(src, panel.at[at, hrows(g)], sems[0], sems[1], partner, c)

    def hand_arrivals(panel, sems):
        ref = panel.at[pl.ds(0, 4)]
        return remote(ref, ref, sems[0], sems[1], partner, c)

    def gather_phase(rowp, colp, own_row, own_col, csems, rsems, first_work, seen, work, between):
        for q in range(4):
            gather_a(rowp, q, 0, own_row, csems).start()
        for g in range(2):
            ring(colp, g, 0, own_col, rsems).start()
            hand(colp, g, 0, own_col, rsems).start()
        for q in range(4):
            gather_b(rowp, q, 0, own_row, csems).start()
        first_work()

        def hop_a(h):
            for q in range(4):
                gather_a_arrival(rowp, q, h, csems).wait_recv()
                if h < 2:
                    gather_a(rowp, q, h + 1, own_row, csems).start()
            for q in range(4):
                gather_b(rowp, q, h + 1, None, csems).start()
            for q in range(4):
                seen(q, col_of(q, mod4(pos_a[q] - ROUTES[q][1] * (h + 1)), pos_b[q]))

        def hop_x(h):
            for g in range(2):
                ring_arrival(colp, g, h, rsems).wait_recv()
                if h < 2:
                    ring(colp, g, h + 1, own_col, rsems).start()
                hand(colp, g, h + 1, own_col, rsems).start()

        def hop_b(i, last):
            for q in range(4):
                gather_b_arrival(rowp, q, i, csems).wait_recv()
                gather_b(rowp, q, i + 4, None, csems, last).start()
            for q in range(4):
                seen(q, arrived_b(q, i))

        hop_a(0)
        hop_b(0, False)
        hop_x(0)
        hop_a(1)
        hop_b(1, False)
        hop_a(2)
        hop_x(1)
        hop_b(2, False)
        hop_b(3, False)
        hop_x(2)
        hop_b(4, True)
        hand_arrivals(colp, rsems).wait_recv()

        @pl.loop(0, 4)
        def _(i):
            for k in range(4):
                work(i * 4 + k)

            @pl.when(i < 3)
            def _():
                hop_b(i + 5, True)

        between()
        gather_last(rowp, csems).wait_recv()

        @pl.loop(8, 12)
        def _(i):
            for q in range(4):
                seen(q, arrived_b(q, i))

    def drain(ref, blocks, sem):
        ref = ref.at[pl.ds(0, blocks)]
        remote(ref, ref, sem, in_sem.at[0], partner, c).wait_send()

    def w_sum(col, rows):
        packed = lists[0, col]
        total = pw[packed & 15, rows, :]
        for j in range(1, 4):
            total = total + pw[lax.shift_right_arithmetic(packed, 4 * j) & 15, rows, :]
        return total

    def y_sum(row, rows):
        packed = lists[1, row]
        total = py[packed & 15, rows, :]
        for j in range(1, 8):
            total = total + py[lax.shift_right_arithmetic(packed, 4 * j) & 15, rows, :]
        return total

    xsem, zsem = (x_s, xf_r), (z_s, zf_r)
    xrsem, zrsem = (xr_s, gp_r.at[0]), (zr_s, gp_r.at[1])

    def start_work():
        for s in range(slots):
            ids[0, s] = left[s]
            ids[1, s] = right[s]
            ids[2, s] = active[s]
        ids[0, slots] = c
        ids[1, slots] = r
        ids[2, slots] = 1

        def packs(which, n):
            @pl.loop(0, n)
            def _(a):
                packed = jnp.int32(0)
                for s in range(slots):
                    ident = left[s] if which == 0 else right[s]
                    packed = jnp.where(ident == a, packed * 16 + (s + 1), packed)
                lists[which, a] = packed

        packs(0, 16)
        packs(1, 8)
        for load in loads[1:]:
            load.wait()

    def w_product(s):
        pw[s + 1] = dot3(tile[s], xcol[ids[1, s]], NN)

    def y_product(s):
        py[s + 1] = dot3(tile[s], xrow[ids[0, s]], TN)

    def scatter_target(q, h, j):
        d = ROUTES[q][1]
        return col_of(q, mod4(pos_a[q] - d * (j + 1)), mod4(pos_b[q] - d * (h + 1)))

    def scatter_b0(q, j):
        return remote(rs0.at[q, j], rsb.at[q, j], w_s, wb_r.at[q, j], r, next_b(q))

    def scatter_b(q, i):
        return remote(rsb.at[q, i], rsb.at[q, i + 4], w_s, wb_r.at[q, i + 4], r, next_b(q))

    def scatter_b_arrival(q, i):
        return remote(rsb.at[q, i], rsb.at[q, i], w_s, wb_r.at[q, i], r, next_b(q))

    def scatter_a(q, h):
        src = rsb.at[q, 8] if h == 0 else rsa.at[q, h - 1]
        return remote(src, rsa.at[q, h], w_s, wa_r.at[q, h], r, next_a(q))

    def scatter_a_arrival(q, h):
        return remote(rsa.at[q, h], rsa.at[q, h], w_s, wa_r.at[q, h], r, next_a(q))

    def scatter_start():
        for j in range(4):
            for q in range(4):
                rs0[q, j] = w_sum(scatter_target(q, 0, j), qrows(q))
            for q in range(4):
                scatter_b0(q, j).start()

    def scatter_hop(h, j):
        i = (h - 1) * 4 + j
        for q in range(4):
            scatter_b_arrival(q, i).wait_recv()
            rsb[q, i] = rsb[q, i] + w_sum(scatter_target(q, h, j), qrows(q))
        if h < 3:
            for q in range(4):
                scatter_b(q, i).start()

    def scatter_step(h):
        for q in range(4):
            scatter_a_arrival(q, h - 1).wait_recv()
            rsa[q, h - 1] = rsa[q, h - 1] + rsb[q, 8 + h]
        for q in range(4):
            scatter_a(q, h).start()

    def y_target(g, h):
        return mod4(x - (1, -1)[g] * (h + 1))

    def y_give(g, h):
        return remote(ys.at[g, h], yx.at[g, h], y_s, yp_r.at[g, h], partner, c)

    def y_ring(g, h):
        src = yx.at[g, 0] if h == 0 else yr.at[g, h - 1]
        return remote(src, yr.at[g, h], y_s, yh_r.at[g, h], next_x(g), c)

    def y_exchange(h):
        for g in range(2):
            ys[g, h] = y_sum(2 * y_target(g, h) + other, hrows(g))
        for g in range(2):
            y_give(g, h).start()

    def y_combine(h):
        for g in range(2):
            y_give(g, h).wait_recv()
            yx[g, h] = yx[g, h] + y_sum(2 * y_target(g, h) + core, hrows(g))
        if h == 0:
            for g in range(2):
                y_ring(g, 0).start()

    def y_hop(h):
        for g in range(2):
            y_ring(g, h - 1).wait_recv()
            yr[g, h - 1] = yr[g, h - 1] + yx[g, h]
            if h < 3:
                y_ring(g, h).start()

    gather_phase(
        xrow, xcol, xt, xt, xsem, xrsem, start_work, lambda q, at: None, w_product, scatter_start
    )

    def y_products(first):
        @pl.loop(0, 4)
        def _(k):
            y_product(jnp.minimum(first + k, slots - 1))

    for j in range(2):
        y_products(8 * j)
        scatter_hop(1, j)
        y_products(8 * j + 4)
    y_exchange(0)
    scatter_hop(2, 0)
    y_exchange(1)
    scatter_hop(1, 2)
    y_exchange(2)
    y_combine(0)
    scatter_hop(2, 1)
    y_exchange(3)
    scatter_hop(1, 3)
    y_combine(1)
    y_combine(2)
    y_combine(3)
    scatter_hop(3, 0)
    for q in range(4):
        scatter_a(q, 0).start()

    @pl.loop(0, 8)
    def _(b):
        xh[b], xl[b] = split(xcol[b])

    eye = lax.broadcasted_iota(jnp.int32, (side, side), 0) == lax.broadcasted_iota(
        jnp.int32, (side, side), 1
    )
    tile[slots] = tile[slots] + jnp.where(eye, STEP_SIZE / jnp.where(eye, tile[slots], 1.0), 0.0)
    scatter_hop(2, 2)
    y_hop(1)
    scatter_hop(3, 1)
    scatter_step(1)
    scatter_hop(2, 3)
    y_hop(2)
    scatter_hop(3, 2)
    scatter_step(2)
    scatter_hop(3, 3)
    y_hop(3)
    for q in range(4):
        scatter_a_arrival(q, 2).wait_recv()
        part = pl.ds((q % 2) * quarter, quarter)
        total = rsa[q, 2] + rsb[q, 11] + yr[q // 2, 2, part, :] + pw[slots + 1, qrows(q), :]
        zrow[c, qrows(q), :] = total
        zcol[r, qrows(q), :] = total

    scale = STEP_SIZE / (2.0 * samp)

    def first_half(s):
        factor = scale * ids[2, s].astype(F32)
        grad = dot3(xrow[ids[0, s]], zcol[ids[1, s]], NT)
        tile[s] = tile[s] - factor * grad

    def seen(q, at):
        zh[at, qrows(q), :], zl[at, qrows(q), :] = split(zrow[at, qrows(q), :])

    def own_seen():
        zh[c], zl[c] = split(zrow[c])

    gather_phase(
        zrow, zcol, zrow.at[c], zcol.at[r], zsem, zrsem, own_seen, seen, first_half, lambda: None
    )

    drain(xrow, 15, x_s)
    drain(xcol, 7, xr_s)
    drain(zrow, 15, z_s)
    drain(zcol, 7, zr_s)
    drain(xrow, 15, w_s)
    drain(xcol, 7, y_s)


def finish(tile, zh, zl, xh, xl, ids, out_hbm, diag_hbm, done, out_sem):
    slots = out_hbm.shape[0]
    side, samp = zh.shape[1:]
    scale = STEP_SIZE / (2.0 * samp)
    dot = functools.partial(lax.dot_general, dimension_numbers=NT, preferred_element_type=F32)

    def stepped(s):
        a, b = ids[0, s], ids[1, s]
        grad = dot(zh[a], xh[b]) + dot(zh[a], xl[b]) + dot(zl[a], xh[b])
        return tile[s] - scale * ids[2, s].astype(F32) * grad

    def out(s):
        return pltpu.make_async_copy(done.at[s], out_hbm.at[s], out_sem.at[s])

    def diag_out():
        return pltpu.make_async_copy(done.at[slots], diag_hbm, out_sem.at[slots])

    eye = lax.broadcasted_iota(jnp.int32, (side, side), 0) == lax.broadcasted_iota(
        jnp.int32, (side, side), 1
    )
    value = stepped(slots)
    done[slots] = jnp.where(eye, value, shrink(value, STEP_SIZE * PENALTY))
    diag_out().start()

    @pl.loop(0, slots)
    def _(s):
        done[s] = shrink(stepped(s), STEP_SIZE * PENALTY * ids[2, s].astype(F32))
        out(s).start()

    diag_out().wait()

    @pl.loop(0, slots)
    def _(s):
        out(s).wait()


def per_device(samples, omega_tiles, omega_diag, tile_rows, tile_cols, tile_active):
    rows, cols = lax.axis_size("row"), lax.axis_size("col")
    samp, side = samples.shape
    slots = omega_tiles.shape[2]
    block = (side, samp)
    dma = pltpu.SemaphoreType.DMA
    vmem = pl.BlockSpec(memory_space=pltpu.VMEM)
    smem = pl.BlockSpec(memory_space=pltpu.SMEM)
    anyw = pl.BlockSpec(memory_space=pl.ANY)
    middle = pl.pallas_call(
        kernel,
        out_shape=(
            pltpu.VMEM((slots + 1, side, side), F32),
            pltpu.VMEM((cols,) + block, BF16),
            pltpu.VMEM((cols,) + block, BF16),
            pltpu.VMEM((rows,) + block, BF16),
            pltpu.VMEM((rows,) + block, BF16),
            pltpu.SMEM((3, slots + 1), jnp.int32),
        ),
        in_specs=[anyw] * 3 + [smem] * 3,
        out_specs=(vmem,) * 5 + (smem,),
        scratch_shapes=[
            pltpu.VMEM((samp, side), F32),
            pltpu.VMEM(block, F32),
            pltpu.VMEM((cols,) + block, F32),
            pltpu.VMEM((rows,) + block, F32),
            pltpu.VMEM((cols,) + block, F32),
            pltpu.VMEM((rows,) + block, F32),
            pltpu.VMEM((slots + 2,) + block, F32),
            pltpu.VMEM((slots + 1,) + block, F32),
            pltpu.VMEM((4, 4, side // 4, samp), F32),
            pltpu.VMEM((4, 12, side // 4, samp), F32),
            pltpu.VMEM((4, 3, side // 4, samp), F32),
            pltpu.VMEM((2, 4, side // 2, samp), F32),
            pltpu.VMEM((2, 4, side // 2, samp), F32),
            pltpu.VMEM((2, 3, side // 2, samp), F32),
            pltpu.SMEM((2, 16), jnp.int32),
            dma((4, 3)), dma((4, 8)), dma(()), dma(()), dma((2, 3)), dma((2,)),
            dma((4, 3)), dma((4, 12)), dma((2, 3)), dma((2, 4)),
            dma(()), dma(()), dma(()), dma(()), dma(()), dma(()), dma((3,)),
        ],
        compiler_params=pltpu.CompilerParams(
            collective_id=0, has_side_effects=True, vmem_limit_bytes=48 * 1024 * 1024
        ),
    )(
        samples,
        omega_tiles.reshape(slots, side, side),
        omega_diag,
        tile_rows.reshape(slots),
        tile_cols.reshape(slots),
        tile_active.reshape(slots),
    )
    new_tiles, new_diag = pl.pallas_call(
        finish,
        out_shape=(
            jax.ShapeDtypeStruct((slots, side, side), F32),
            jax.ShapeDtypeStruct((side, side), F32),
        ),
        in_specs=[vmem] * 5 + [smem],
        out_specs=(anyw, anyw),
        scratch_shapes=[pltpu.VMEM((slots + 1, side, side), F32), dma((slots + 1,))],
        compiler_params=pltpu.CompilerParams(vmem_limit_bytes=16 * 1024 * 1024),
    )(*middle)
    return new_tiles[None, None], new_diag


def solution(mesh):
    in_specs = (
        P(None, ("row", "col")),
        P("row", "col", None, None, None),
        P(("row", "col"), None),
        P("row", "col", None),
        P("row", "col", None),
        P("row", "col", None),
    )
    out_specs = (P("row", "col", None, None, None), P(("row", "col"), None))
    return jax.shard_map(
        per_device, mesh=mesh, in_specs=in_specs, out_specs=out_specs, check_vma=False
    )
```

```python
import functools

import jax
import jax.numpy as jnp
from jax import lax
from jax.experimental import pallas as pl
from jax.experimental.pallas import tpu as pltpu
from jax.sharding import PartitionSpec as P

MESH = pl.DeviceIdType.MESH
F32 = jnp.float32
BF16 = jnp.bfloat16
STEP_SIZE = 0.05
PENALTY = 4.0
SIDE = 4
NN = (((1,), (0,)), ((), ()))
NT = (((1,), (1,)), ((), ()))
TN = (((0,), (0,)), ((), ()))
ROUTES = ((True, 1), (True, -1), (False, 1), (False, -1))


def split(v):
    high = v.astype(BF16)
    low = (v - high.astype(F32)).astype(BF16)
    return high, low


def dot3(a, b, dims):
    ah, al = split(a)
    bh, bl = split(b)
    dot = functools.partial(lax.dot_general, dimension_numbers=dims, preferred_element_type=F32)
    return dot(ah, bh) + dot(ah, bl) + dot(al, bh)


def mod4(v):
    return lax.rem(v + 2 * SIDE, SIDE)


def shrink(v, limit):
    return jnp.where(v > 0, 1.0, -1.0) * jnp.maximum(jnp.abs(v) - limit, 0.0)


def kernel(
    samples_hbm, tiles_hbm, diag_hbm, left, right, active,
    tile, zh, zl, xh, xl, ids,
    raw, xt, xrow, xcol, zrow, zcol, pw, py, rs0, rsb, rsa, ys, yx, yr, lists,
    ga_r, gb_r, xf_r, zf_r, gh_r, gp_r, wa_r, wb_r, yh_r, yp_r,
    x_s, xr_s, z_s, zr_s, w_s, y_s, in_sem,
):
    slots = left.shape[0]
    samp, side = raw.shape
    quarter, half = side // 4, side // 2
    r = lax.axis_index("row")
    c = lax.axis_index("col")
    x, core = lax.div(r, 2), lax.rem(r, 2)
    yy, zz = lax.div(c, SIDE), lax.rem(c, SIDE)
    other = 1 - core
    partner = 2 * x + other
    pos_a = [zz if first else yy for first, _ in ROUTES]
    pos_b = [yy if first else zz for first, _ in ROUTES]

    def col_of(q, a, b):
        return b * SIDE + a if ROUTES[q][0] else a * SIDE + b

    def qrows(q):
        return pl.ds(q * quarter, quarter)

    def hrows(g):
        return pl.ds(g * half, half)

    def remote(src, dst, send, recv, row, col):
        return pltpu.make_async_remote_copy(
            src_ref=src, dst_ref=dst, send_sem=send, recv_sem=recv,
            device_id=(row, col), device_id_type=MESH,
        )

    def next_a(q):
        return col_of(q, mod4(pos_a[q] + ROUTES[q][1]), pos_b[q])

    def next_b(q):
        return col_of(q, pos_a[q], mod4(pos_b[q] + ROUTES[q][1]))

    def next_x(g):
        return 2 * mod4(x + (1, -1)[g]) + core

    barrier = pltpu.get_barrier_semaphore()
    peers = [(r, next_a(q)) for q in range(4)]
    peers += [(next_x(0), c), (next_x(1), c), (partner, c)]
    for row, col in peers:
        pl.semaphore_signal(barrier, inc=1, device_id=(row, col), device_id_type=MESH)
    loads = [
        pltpu.make_async_copy(samples_hbm, raw, in_sem.at[0]),
        pltpu.make_async_copy(tiles_hbm, tile.at[pl.ds(0, slots)], in_sem.at[1]),
        pltpu.make_async_copy(diag_hbm, tile.at[slots], in_sem.at[2]),
    ]
    for load in loads:
        load.start()
    loads[0].wait()
    own = raw[...].T
    xt[...] = own
    xrow[c] = own
    xcol[r] = own
    pw[0] = jnp.zeros((side, samp), F32)
    py[0] = jnp.zeros((side, samp), F32)
    pl.semaphore_wait(barrier, len(peers))

    def gather_a(panel, q, h, own, sems):
        d = ROUTES[q][1]
        at = col_of(q, mod4(pos_a[q] - d * h), pos_b[q])
        src = own.at[qrows(q)] if h == 0 else panel.at[at, qrows(q)]
        return remote(src, panel.at[at, qrows(q)], sems[0], ga_r.at[q, h], r, next_a(q))

    def gather_a_arrival(panel, q, h, sems):
        d = ROUTES[q][1]
        at = col_of(q, mod4(pos_a[q] - d * (h + 1)), pos_b[q])
        ref = panel.at[at, qrows(q)]
        return remote(ref, ref, sems[0], ga_r.at[q, h], r, next_a(q))

    def gather_b(panel, q, i, own, sems, last=False):
        d = ROUTES[q][1]
        at = col_of(q, mod4(pos_a[q] - d * lax.rem(i, 4)), mod4(pos_b[q] - d * lax.div(i, 4)))
        src = panel.at[at, qrows(q)] if own is None else own.at[qrows(q)]
        recv = sems[1] if last else gb_r.at[q, i]
        return remote(src, panel.at[at, qrows(q)], sems[0], recv, r, next_b(q))

    def arrived_b(q, i):
        d = ROUTES[q][1]
        return col_of(q, mod4(pos_a[q] - d * lax.rem(i, 4)), mod4(pos_b[q] - d * (lax.div(i, 4) + 1)))

    def gather_b_arrival(panel, q, i, sems):
        ref = panel.at[arrived_b(q, i), qrows(q)]
        return remote(ref, ref, sems[0], gb_r.at[q, i], r, next_b(q))

    def gather_last(panel, sems):
        ref = panel.at[pl.ds(0, 4)]
        return remote(ref, ref, sems[0], sems[1], r, next_b(0))

    def ring(panel, g, h, own, sems):
        at = 2 * mod4(x - (1, -1)[g] * h) + core
        src = own.at[hrows(g)] if h == 0 else panel.at[at, hrows(g)]
        return remote(src, panel.at[at, hrows(g)], sems[0], gh_r.at[g, h], next_x(g), c)

    def ring_arrival(panel, g, h, sems):
        at = 2 * mod4(x - (1, -1)[g] * (h + 1)) + core
        ref = panel.at[at, hrows(g)]
        return remote(ref, ref, sems[0], gh_r.at[g, h], next_x(g), c)

    def hand(panel, g, h, own, sems):
        at = 2 * mod4(x - (1, -1)[g] * h) + core
        src = own.at[hrows(g)] if h == 0 else panel.at[at, hrows(g)]
        return remote(src, panel.at[at, hrows(g)], sems[0], sems[1], partner, c)

    def hand_arrivals(panel, sems):
        ref = panel.at[pl.ds(0, 4)]
        return remote(ref, ref, sems[0], sems[1], partner, c)

    def gather_phase(rowp, colp, own_row, own_col, csems, rsems, first_work, seen, work, between):
        for q in range(4):
            gather_a(rowp, q, 0, own_row, csems).start()
        for g in range(2):
            ring(colp, g, 0, own_col, rsems).start()
            hand(colp, g, 0, own_col, rsems).start()
        for q in range(4):
            gather_b(rowp, q, 0, own_row, csems).start()
        first_work()

        def hop_a(h):
            for q in range(4):
                gather_a_arrival(rowp, q, h, csems).wait_recv()
                if h < 2:
                    gather_a(rowp, q, h + 1, own_row, csems).start()
            for q in range(4):
                gather_b(rowp, q, h + 1, None, csems).start()
            for q in range(4):
                seen(q, col_of(q, mod4(pos_a[q] - ROUTES[q][1] * (h + 1)), pos_b[q]))

        def hop_x(h):
            for g in range(2):
                ring_arrival(colp, g, h, rsems).wait_recv()
                if h < 2:
                    ring(colp, g, h + 1, own_col, rsems).start()
                hand(colp, g, h + 1, own_col, rsems).start()

        def hop_b(i, last):
            for q in range(4):
                gather_b_arrival(rowp, q, i, csems).wait_recv()
                gather_b(rowp, q, i + 4, None, csems, last).start()
            for q in range(4):
                seen(q, arrived_b(q, i))

        hop_a(0)
        hop_b(0, False)
        hop_x(0)
        hop_a(1)
        hop_b(1, False)
        hop_a(2)
        hop_x(1)
        hop_b(2, False)
        hop_b(3, False)
        hop_x(2)
        hop_b(4, True)
        hand_arrivals(colp, rsems).wait_recv()

        @pl.loop(0, 4)
        def _(i):
            for k in range(4):
                work(i * 4 + k)

            @pl.when(i < 3)
            def _():
                hop_b(i + 5, True)

        between()
        gather_last(rowp, csems).wait_recv()

        @pl.loop(8, 12)
        def _(i):
            for q in range(4):
                seen(q, arrived_b(q, i))

    def drain(ref, blocks, sem):
        ref = ref.at[pl.ds(0, blocks)]
        remote(ref, ref, sem, in_sem.at[0], partner, c).wait_send()

    def w_sum(col, rows):
        packed = lists[0, col]
        total = pw[packed & 15, rows, :]
        for j in range(1, 4):
            total = total + pw[lax.shift_right_arithmetic(packed, 4 * j) & 15, rows, :]
        return total

    def y_sum(row, rows):
        packed = lists[1, row]
        total = py[packed & 15, rows, :]
        for j in range(1, 8):
            total = total + py[lax.shift_right_arithmetic(packed, 4 * j) & 15, rows, :]
        return total

    xsem, zsem = (x_s, xf_r), (z_s, zf_r)
    xrsem, zrsem = (xr_s, gp_r.at[0]), (zr_s, gp_r.at[1])

    def start_work():
        for s in range(slots):
            ids[0, s] = left[s]
            ids[1, s] = right[s]
            ids[2, s] = active[s]
        ids[0, slots] = c
        ids[1, slots] = r
        ids[2, slots] = 1

        def packs(which, n):
            @pl.loop(0, n)
            def _(a):
                packed = jnp.int32(0)
                for s in range(slots):
                    ident = left[s] if which == 0 else right[s]
                    packed = jnp.where(ident == a, packed * 16 + (s + 1), packed)
                lists[which, a] = packed

        packs(0, 16)
        packs(1, 8)
        for load in loads[1:]:
            load.wait()

    def w_product(s):
        pw[s + 1] = dot3(tile[s], xcol[ids[1, s]], NN)

    def y_product(s):
        py[s + 1] = dot3(tile[s], xrow[ids[0, s]], TN)

    def scatter_target(q, h, j):
        d = ROUTES[q][1]
        return col_of(q, mod4(pos_a[q] - d * (j + 1)), mod4(pos_b[q] - d * (h + 1)))

    def scatter_b0(q, j):
        return remote(rs0.at[q, j], rsb.at[q, j], w_s, wb_r.at[q, j], r, next_b(q))

    def scatter_b(q, i):
        return remote(rsb.at[q, i], rsb.at[q, i + 4], w_s, wb_r.at[q, i + 4], r, next_b(q))

    def scatter_b_arrival(q, i):
        return remote(rsb.at[q, i], rsb.at[q, i], w_s, wb_r.at[q, i], r, next_b(q))

    def scatter_a(q, h):
        src = rsb.at[q, 8] if h == 0 else rsa.at[q, h - 1]
        return remote(src, rsa.at[q, h], w_s, wa_r.at[q, h], r, next_a(q))

    def scatter_a_arrival(q, h):
        return remote(rsa.at[q, h], rsa.at[q, h], w_s, wa_r.at[q, h], r, next_a(q))

    def scatter_start():
        for j in range(4):
            for q in range(4):
                rs0[q, j] = w_sum(scatter_target(q, 0, j), qrows(q))
            for q in range(4):
                scatter_b0(q, j).start()

    def scatter_hop(h, j):
        i = (h - 1) * 4 + j
        for q in range(4):
            scatter_b_arrival(q, i).wait_recv()
            rsb[q, i] = rsb[q, i] + w_sum(scatter_target(q, h, j), qrows(q))
        if h < 3:
            for q in range(4):
                scatter_b(q, i).start()

    def scatter_step(h):
        for q in range(4):
            scatter_a_arrival(q, h - 1).wait_recv()
            rsa[q, h - 1] = rsa[q, h - 1] + rsb[q, 8 + h]
        for q in range(4):
            scatter_a(q, h).start()

    def y_target(g, h):
        return mod4(x - (1, -1)[g] * (h + 1))

    def y_give(g, h):
        return remote(ys.at[g, h], yx.at[g, h], y_s, yp_r.at[g, h], partner, c)

    def y_ring(g, h):
        src = yx.at[g, 0] if h == 0 else yr.at[g, h - 1]
        return remote(src, yr.at[g, h], y_s, yh_r.at[g, h], next_x(g), c)

    def y_exchange(h):
        for g in range(2):
            ys[g, h] = y_sum(2 * y_target(g, h) + other, hrows(g))
        for g in range(2):
            y_give(g, h).start()

    def y_combine(h):
        for g in range(2):
            y_give(g, h).wait_recv()
            yx[g, h] = yx[g, h] + y_sum(2 * y_target(g, h) + core, hrows(g))
        if h == 0:
            for g in range(2):
                y_ring(g, 0).start()

    def y_hop(h):
        for g in range(2):
            y_ring(g, h - 1).wait_recv()
            yr[g, h - 1] = yr[g, h - 1] + yx[g, h]
            if h < 3:
                y_ring(g, h).start()

    gather_phase(
        xrow, xcol, xt, xt, xsem, xrsem, start_work, lambda q, at: None, w_product, scatter_start
    )

    def y_products(first):
        @pl.loop(0, 4)
        def _(k):
            y_product(jnp.minimum(first + k, slots - 1))

    for j in range(2):
        y_products(8 * j)
        scatter_hop(1, j)
        y_products(8 * j + 4)
    y_exchange(0)
    scatter_hop(2, 0)
    y_exchange(1)
    scatter_hop(1, 2)
    y_exchange(2)
    y_combine(0)
    scatter_hop(2, 1)
    y_exchange(3)
    scatter_hop(1, 3)
    y_combine(1)
    y_combine(2)
    y_combine(3)
    scatter_hop(3, 0)
    for q in range(4):
        scatter_a(q, 0).start()

    @pl.loop(0, 8)
    def _(b):
        xh[b], xl[b] = split(xcol[b].T)

    eye = lax.broadcasted_iota(jnp.int32, (side, side), 0) == lax.broadcasted_iota(
        jnp.int32, (side, side), 1
    )
    tile[slots] = tile[slots] + jnp.where(eye, STEP_SIZE / jnp.where(eye, tile[slots], 1.0), 0.0)
    scatter_hop(2, 2)
    y_hop(1)
    scatter_hop(3, 1)
    scatter_step(1)
    scatter_hop(2, 3)
    y_hop(2)
    scatter_hop(3, 2)
    scatter_step(2)
    scatter_hop(3, 3)
    y_hop(3)
    for q in range(4):
        scatter_a_arrival(q, 2).wait_recv()
        part = pl.ds((q % 2) * quarter, quarter)
        total = rsa[q, 2] + rsb[q, 11] + yr[q // 2, 2, part, :] + pw[slots + 1, qrows(q), :]
        zrow[c, qrows(q), :] = total
        zcol[r, qrows(q), :] = total

    scale = STEP_SIZE / (2.0 * samp)

    def first_half(s):
        factor = scale * ids[2, s].astype(F32)
        grad = dot3(xrow[ids[0, s]], zcol[ids[1, s]], NT)
        tile[s] = tile[s] - factor * grad

    def seen(q, at):
        zh[at, qrows(q), :], zl[at, qrows(q), :] = split(zrow[at, qrows(q), :])

    def own_seen():
        zh[c], zl[c] = split(zrow[c])

    gather_phase(
        zrow, zcol, zrow.at[c], zcol.at[r], zsem, zrsem, own_seen, seen, first_half, lambda: None
    )

    drain(xrow, 15, x_s)
    drain(xcol, 7, xr_s)
    drain(zrow, 15, z_s)
    drain(zcol, 7, zr_s)
    drain(xrow, 15, w_s)
    drain(xcol, 7, y_s)


def finish(tile, zh, zl, xh, xl, ids, out_hbm, diag_hbm, done, out_sem):
    slots = out_hbm.shape[0]
    side, samp = zh.shape[1:]
    scale = STEP_SIZE / (2.0 * samp)
    dot = functools.partial(lax.dot_general, dimension_numbers=NN, preferred_element_type=F32)

    def stepped(s):
        a, b = ids[0, s], ids[1, s]
        grad = dot(zh[a], xh[b]) + dot(zh[a], xl[b]) + dot(zl[a], xh[b])
        return tile[s] - scale * ids[2, s].astype(F32) * grad

    def out(s):
        return pltpu.make_async_copy(done.at[s], out_hbm.at[s], out_sem)

    def diag_out():
        return pltpu.make_async_copy(done.at[slots], diag_hbm, out_sem)

    eye = lax.broadcasted_iota(jnp.int32, (side, side), 0) == lax.broadcasted_iota(
        jnp.int32, (side, side), 1
    )
    value = stepped(slots)
    done[slots] = jnp.where(eye, value, shrink(value, STEP_SIZE * PENALTY))
    diag_out().start()

    for s in range(slots):
        done[s] = shrink(stepped(s), STEP_SIZE * PENALTY * ids[2, s].astype(F32))
        out(s).start()

    pltpu.make_async_copy(done, done, out_sem).wait()


def per_device(samples, omega_tiles, omega_diag, tile_rows, tile_cols, tile_active):
    rows, cols = lax.axis_size("row"), lax.axis_size("col")
    samp, side = samples.shape
    slots = omega_tiles.shape[2]
    block = (side, samp)
    dma = pltpu.SemaphoreType.DMA
    vmem = pl.BlockSpec(memory_space=pltpu.VMEM)
    smem = pl.BlockSpec(memory_space=pltpu.SMEM)
    anyw = pl.BlockSpec(memory_space=pl.ANY)
    middle = pl.pallas_call(
        kernel,
        out_shape=(
            pltpu.VMEM((slots + 1, side, side), F32),
            pltpu.VMEM((cols,) + block, BF16),
            pltpu.VMEM((cols,) + block, BF16),
            pltpu.VMEM((rows, samp, side), BF16),
            pltpu.VMEM((rows, samp, side), BF16),
            pltpu.SMEM((3, slots + 1), jnp.int32),
        ),
        in_specs=[anyw] * 3 + [smem] * 3,
        out_specs=(vmem,) * 5 + (smem,),
        scratch_shapes=[
            pltpu.VMEM((samp, side), F32),
            pltpu.VMEM(block, F32),
            pltpu.VMEM((cols,) + block, F32),
            pltpu.VMEM((rows,) + block, F32),
            pltpu.VMEM((cols,) + block, F32),
            pltpu.VMEM((rows,) + block, F32),
            pltpu.VMEM((slots + 2,) + block, F32),
            pltpu.VMEM((slots + 1,) + block, F32),
            pltpu.VMEM((4, 4, side // 4, samp), F32),
            pltpu.VMEM((4, 12, side // 4, samp), F32),
            pltpu.VMEM((4, 3, side // 4, samp), F32),
            pltpu.VMEM((2, 4, side // 2, samp), F32),
            pltpu.VMEM((2, 4, side // 2, samp), F32),
            pltpu.VMEM((2, 3, side // 2, samp), F32),
            pltpu.SMEM((2, 16), jnp.int32),
            dma((4, 3)), dma((4, 8)), dma(()), dma(()), dma((2, 3)), dma((2,)),
            dma((4, 3)), dma((4, 12)), dma((2, 3)), dma((2, 4)),
            dma(()), dma(()), dma(()), dma(()), dma(()), dma(()), dma((3,)),
        ],
        compiler_params=pltpu.CompilerParams(
            collective_id=0, has_side_effects=True, vmem_limit_bytes=48 * 1024 * 1024
        ),
    )(
        samples,
        omega_tiles.reshape(slots, side, side),
        omega_diag,
        tile_rows.reshape(slots),
        tile_cols.reshape(slots),
        tile_active.reshape(slots),
    )
    new_tiles, new_diag = pl.pallas_call(
        finish,
        out_shape=(
            jax.ShapeDtypeStruct((slots, side, side), F32),
            jax.ShapeDtypeStruct((side, side), F32),
        ),
        in_specs=[vmem] * 5 + [smem],
        out_specs=(anyw, anyw),
        scratch_shapes=[pltpu.VMEM((slots + 1, side, side), F32), dma(())],
        compiler_params=pltpu.CompilerParams(vmem_limit_bytes=16 * 1024 * 1024),
    )(*middle)
    return new_tiles[None, None], new_diag


def solution(mesh):
    in_specs = (
        P(None, ("row", "col")),
        P("row", "col", None, None, None),
        P(("row", "col"), None),
        P("row", "col", None),
        P("row", "col", None),
        P("row", "col", None),
    )
    out_specs = (P("row", "col", None, None, None), P(("row", "col"), None))
    return jax.shard_map(
        per_device, mesh=mesh, in_specs=in_specs, out_specs=out_specs, check_vma=False
    )
```

```python
import functools

import jax
import jax.numpy as jnp
from jax import lax
from jax.experimental import pallas as pl
from jax.experimental.pallas import tpu as pltpu
from jax.sharding import PartitionSpec as P

MESH = pl.DeviceIdType.MESH
F32 = jnp.float32
BF16 = jnp.bfloat16
STEP_SIZE = 0.05
PENALTY = 4.0
SIDE = 4
NN = (((1,), (0,)), ((), ()))
NT = (((1,), (1,)), ((), ()))
TN = (((0,), (0,)), ((), ()))
ROUTES = ((True, 1), (True, -1), (False, 1), (False, -1))


def split(v):
    high = v.astype(BF16)
    low = (v - high.astype(F32)).astype(BF16)
    return high, low


def dot3(a, b, dims):
    ah, al = split(a)
    bh, bl = split(b)
    dot = functools.partial(lax.dot_general, dimension_numbers=dims, preferred_element_type=F32)
    return dot(ah, bh) + dot(ah, bl) + dot(al, bh)


def mod4(v):
    return lax.rem(v + 2 * SIDE, SIDE)


def shrink(v, limit):
    return jnp.where(v > 0, 1.0, -1.0) * jnp.maximum(jnp.abs(v) - limit, 0.0)


def kernel(
    samples_hbm, tiles_hbm, diag_hbm, left_hbm, right_hbm, active_hbm,
    tile, zh, zl, xh, xl, ids,
    raw, xt, xrow, xcol, zrow, zcol, pw, py, rs0, rsb, rsa, ys, yx, yr, lists, idv0, idv1, idv2, idv, named,
    ga_r, gb_r, xf_r, zf_r, gh_r, gp_r, wa_r, wb_r, yh_r, yp_r,
    x_s, xr_s, z_s, zr_s, w_s, y_s, in_sem,
):
    slots = left_hbm.shape[0]
    samp, side = raw.shape
    quarter, half = side // 4, side // 2
    r = lax.axis_index("row")
    c = lax.axis_index("col")
    x, core = lax.div(r, 2), lax.rem(r, 2)
    yy, zz = lax.div(c, SIDE), lax.rem(c, SIDE)
    other = 1 - core
    partner = 2 * x + other
    pos_a = [zz if first else yy for first, _ in ROUTES]
    pos_b = [yy if first else zz for first, _ in ROUTES]

    def col_of(q, a, b):
        return b * SIDE + a if ROUTES[q][0] else a * SIDE + b

    def qrows(q):
        return pl.ds(q * quarter, quarter)

    def hrows(g):
        return pl.ds(g * half, half)

    def remote(src, dst, send, recv, row, col):
        return pltpu.make_async_remote_copy(
            src_ref=src, dst_ref=dst, send_sem=send, recv_sem=recv,
            device_id=(row, col), device_id_type=MESH,
        )

    def next_a(q):
        return col_of(q, mod4(pos_a[q] + ROUTES[q][1]), pos_b[q])

    def next_b(q):
        return col_of(q, pos_a[q], mod4(pos_b[q] + ROUTES[q][1]))

    def next_x(g):
        return 2 * mod4(x + (1, -1)[g]) + core

    barrier = pltpu.get_barrier_semaphore()
    peers = [(r, next_a(q)) for q in range(4)]
    peers += [(next_x(0), c), (next_x(1), c), (partner, c)]
    for row, col in peers:
        pl.semaphore_signal(barrier, inc=1, device_id=(row, col), device_id_type=MESH)
    loads = [
        pltpu.make_async_copy(samples_hbm, raw, in_sem.at[0]),
        pltpu.make_async_copy(tiles_hbm, tile.at[pl.ds(0, slots)], in_sem.at[1]),
        pltpu.make_async_copy(diag_hbm, tile.at[slots], in_sem.at[2]),
        pltpu.make_async_copy(left_hbm, idv0, in_sem.at[3]),
        pltpu.make_async_copy(right_hbm, idv1, in_sem.at[4]),
        pltpu.make_async_copy(active_hbm, idv2, in_sem.at[5]),
    ]
    for load in loads:
        load.start()
    loads[0].wait()
    own = raw[...].T
    xt[...] = own
    xrow[c] = own
    xcol[r] = own
    pw[0] = jnp.zeros((side, samp), F32)
    py[0] = jnp.zeros((side, samp), F32)
    pl.semaphore_wait(barrier, len(peers))

    def gather_a(panel, q, h, own, sems):
        d = ROUTES[q][1]
        at = col_of(q, mod4(pos_a[q] - d * h), pos_b[q])
        src = own.at[qrows(q)] if h == 0 else panel.at[at, qrows(q)]
        return remote(src, panel.at[at, qrows(q)], sems[0], ga_r.at[q, h], r, next_a(q))

    def gather_a_arrival(panel, q, h, sems):
        d = ROUTES[q][1]
        at = col_of(q, mod4(pos_a[q] - d * (h + 1)), pos_b[q])
        ref = panel.at[at, qrows(q)]
        return remote(ref, ref, sems[0], ga_r.at[q, h], r, next_a(q))

    def gather_b(panel, q, i, own, sems, last=False):
        d = ROUTES[q][1]
        at = col_of(q, mod4(pos_a[q] - d * lax.rem(i, 4)), mod4(pos_b[q] - d * lax.div(i, 4)))
        src = panel.at[at, qrows(q)] if own is None else own.at[qrows(q)]
        recv = sems[1] if last else gb_r.at[q, i]
        return remote(src, panel.at[at, qrows(q)], sems[0], recv, r, next_b(q))

    def arrived_b(q, i):
        d = ROUTES[q][1]
        return col_of(q, mod4(pos_a[q] - d * lax.rem(i, 4)), mod4(pos_b[q] - d * (lax.div(i, 4) + 1)))

    def gather_b_arrival(panel, q, i, sems):
        ref = panel.at[arrived_b(q, i), qrows(q)]
        return remote(ref, ref, sems[0], gb_r.at[q, i], r, next_b(q))

    def gather_last(panel, sems):
        ref = panel.at[pl.ds(0, 4)]
        return remote(ref, ref, sems[0], sems[1], r, next_b(0))

    def ring(panel, g, h, own, sems):
        at = 2 * mod4(x - (1, -1)[g] * h) + core
        src = own.at[hrows(g)] if h == 0 else panel.at[at, hrows(g)]
        return remote(src, panel.at[at, hrows(g)], sems[0], gh_r.at[g, h], next_x(g), c)

    def ring_arrival(panel, g, h, sems):
        at = 2 * mod4(x - (1, -1)[g] * (h + 1)) + core
        ref = panel.at[at, hrows(g)]
        return remote(ref, ref, sems[0], gh_r.at[g, h], next_x(g), c)

    def hand(panel, g, h, own, sems):
        at = 2 * mod4(x - (1, -1)[g] * h) + core
        src = own.at[hrows(g)] if h == 0 else panel.at[at, hrows(g)]
        return remote(src, panel.at[at, hrows(g)], sems[0], sems[1], partner, c)

    def hand_arrivals(panel, sems):
        ref = panel.at[pl.ds(0, 4)]
        return remote(ref, ref, sems[0], sems[1], partner, c)

    def gather_phase(rowp, colp, own_row, own_col, csems, rsems, first_work, seen, work, early, between):
        for q in range(4):
            gather_a(rowp, q, 0, own_row, csems).start()
        for g in range(2):
            ring(colp, g, 0, own_col, rsems).start()
            hand(colp, g, 0, own_col, rsems).start()
        for q in range(4):
            gather_b(rowp, q, 0, own_row, csems).start()
        first_work()

        def hop_a(h):
            for q in range(4):
                gather_a_arrival(rowp, q, h, csems).wait_recv()
                if h < 2:
                    gather_a(rowp, q, h + 1, own_row, csems).start()
            for q in range(4):
                gather_b(rowp, q, h + 1, None, csems).start()
            for q in range(4):
                seen(q, col_of(q, mod4(pos_a[q] - ROUTES[q][1] * (h + 1)), pos_b[q]))

        def hop_x(h):
            for g in range(2):
                ring_arrival(colp, g, h, rsems).wait_recv()
                if h < 2:
                    ring(colp, g, h + 1, own_col, rsems).start()
                hand(colp, g, h + 1, own_col, rsems).start()

        def hop_b(i, last):
            for q in range(4):
                gather_b_arrival(rowp, q, i, csems).wait_recv()
                gather_b(rowp, q, i + 4, None, csems, last).start()
            for q in range(4):
                seen(q, arrived_b(q, i))

        def works(first, last):
            @pl.loop(first // 4, last // 4)
            def _(i):
                for k in range(4):
                    work(i * 4 + k)

        hop_a(0)
        hop_b(0, False)
        hop_a(1)
        hop_x(0)
        hop_b(1, False)
        hop_a(2)
        hop_b(2, False)
        hop_x(1)
        hop_b(3, False)
        hop_b(4, True)
        hop_b(5, True)
        hop_x(2)
        hop_b(6, True)
        hand_arrivals(colp, rsems).wait_recv()
        works(0, early)
        hop_b(7, True)
        works(early, 16)
        between()
        gather_last(rowp, csems).wait_recv()

        @pl.loop(8, 12)
        def _(i):
            for q in range(4):
                seen(q, arrived_b(q, i))

    def drain(ref, blocks, sem):
        ref = ref.at[pl.ds(0, blocks)]
        remote(ref, ref, sem, in_sem.at[0], partner, c).wait_send()

    def w_sum(col, rows):
        packed = lists[0, col]
        total = pw[packed & 15, rows, :]
        for j in range(1, 4):
            total = total + pw[lax.shift_right_arithmetic(packed, 4 * j) & 15, rows, :]
        return total

    def y_sum(row, rows):
        packed = lists[1, row]
        total = py[packed & 15, rows, :]
        for j in range(1, 8):
            total = total + py[lax.shift_right_arithmetic(packed, 4 * j) & 15, rows, :]
        return total

    xsem, zsem = (x_s, xf_r), (z_s, zf_r)
    xrsem, zrsem = (xr_s, gp_r.at[0]), (zr_s, gp_r.at[1])

    def start_work():
        for load in loads[3:]:
            load.wait()
        for k, ref in enumerate((idv0, idv1, idv2)):
            idv[pl.ds(k, 1), pl.ds(0, slots)] = ref[...].reshape(1, slots)
        move = pltpu.make_async_copy(idv, named, in_sem.at[6])
        move.start()
        move.wait()
        for s in range(slots):
            for k in range(3):
                ids[k, s] = named[k, s]
        ids[0, slots] = c
        ids[1, slots] = r
        ids[2, slots] = 1

        def packs(which, n):
            @pl.loop(0, n)
            def _(a):
                packed = jnp.int32(0)
                for s in range(slots):
                    ident = named[which, s]
                    packed = jnp.where(ident == a, packed * 16 + (s + 1), packed)
                lists[which, a] = packed

        packs(0, 16)
        packs(1, 8)
        for load in loads[1:3]:
            load.wait()

    def w_product(s):
        pw[s + 1] = dot3(tile[s], xcol[ids[1, s]], NN)

    def y_product(s):
        py[s + 1] = dot3(tile[s], xrow[ids[0, s]], TN)

    def scatter_target(q, h, j):
        d = ROUTES[q][1]
        return col_of(q, mod4(pos_a[q] - d * (j + 1)), mod4(pos_b[q] - d * (h + 1)))

    def scatter_b0(q, j):
        return remote(rs0.at[q, j], rsb.at[q, j], w_s, wb_r.at[q, j], r, next_b(q))

    def scatter_b(q, i):
        return remote(rsb.at[q, i], rsb.at[q, i + 4], w_s, wb_r.at[q, i + 4], r, next_b(q))

    def scatter_b_arrival(q, i):
        return remote(rsb.at[q, i], rsb.at[q, i], w_s, wb_r.at[q, i], r, next_b(q))

    def scatter_a(q, h):
        src = rsb.at[q, 8] if h == 0 else rsa.at[q, h - 1]
        return remote(src, rsa.at[q, h], w_s, wa_r.at[q, h], r, next_a(q))

    def scatter_a_arrival(q, h):
        return remote(rsa.at[q, h], rsa.at[q, h], w_s, wa_r.at[q, h], r, next_a(q))

    def scatter_start():
        for j in range(4):
            for q in range(4):
                rs0[q, j] = w_sum(scatter_target(q, 0, j), qrows(q))
            for q in range(4):
                scatter_b0(q, j).start()

    def scatter_hop(h, j):
        i = (h - 1) * 4 + j
        for q in range(4):
            scatter_b_arrival(q, i).wait_recv()
            rsb[q, i] = rsb[q, i] + w_sum(scatter_target(q, h, j), qrows(q))
        if h < 3:
            for q in range(4):
                scatter_b(q, i).start()

    def scatter_step(h):
        for q in range(4):
            scatter_a_arrival(q, h - 1).wait_recv()
            rsa[q, h - 1] = rsa[q, h - 1] + rsb[q, 8 + h]
        for q in range(4):
            scatter_a(q, h).start()

    def y_target(g, h):
        return mod4(x - (1, -1)[g] * (h + 1))

    def y_give(g, h):
        return remote(ys.at[g, h], yx.at[g, h], y_s, yp_r.at[g, h], partner, c)

    def y_ring(g, h):
        src = yx.at[g, 0] if h == 0 else yr.at[g, h - 1]
        return remote(src, yr.at[g, h], y_s, yh_r.at[g, h], next_x(g), c)

    def y_exchange(h):
        for g in range(2):
            ys[g, h] = y_sum(2 * y_target(g, h) + other, hrows(g))
        for g in range(2):
            y_give(g, h).start()

    def y_combine(h):
        for g in range(2):
            y_give(g, h).wait_recv()
            yx[g, h] = yx[g, h] + y_sum(2 * y_target(g, h) + core, hrows(g))
        if h == 0:
            for g in range(2):
                y_ring(g, 0).start()

    def y_hop(h):
        for g in range(2):
            y_ring(g, h - 1).wait_recv()
            yr[g, h - 1] = yr[g, h - 1] + yx[g, h]
            if h < 3:
                y_ring(g, h).start()

    gather_phase(
        xrow, xcol, xt, xt, xsem, xrsem, start_work, lambda q, at: None, w_product, 8, scatter_start
    )

    def y_products(first):
        @pl.loop(0, 4)
        def _(k):
            y_product(jnp.minimum(first + k, slots - 1))

    for j in range(2):
        y_products(8 * j)
        scatter_hop(1, j)
        y_products(8 * j + 4)
    y_exchange(0)
    scatter_hop(2, 0)
    y_exchange(1)
    scatter_hop(1, 2)
    y_exchange(2)
    y_combine(0)
    scatter_hop(2, 1)
    y_exchange(3)
    scatter_hop(1, 3)
    y_combine(1)
    y_combine(2)
    y_combine(3)
    scatter_hop(3, 0)
    for q in range(4):
        scatter_a(q, 0).start()

    @pl.loop(0, 8)
    def _(b):
        xh[b], xl[b] = split(xcol[b].T)

    eye = lax.broadcasted_iota(jnp.int32, (side, side), 0) == lax.broadcasted_iota(
        jnp.int32, (side, side), 1
    )
    tile[slots] = tile[slots] + jnp.where(eye, STEP_SIZE / jnp.where(eye, tile[slots], 1.0), 0.0)
    scatter_hop(2, 2)
    y_hop(1)
    scatter_hop(3, 1)
    scatter_step(1)
    scatter_hop(2, 3)
    y_hop(2)
    scatter_hop(3, 2)
    scatter_step(2)
    scatter_hop(3, 3)
    y_hop(3)
    for q in range(4):
        scatter_a_arrival(q, 2).wait_recv()
        part = pl.ds((q % 2) * quarter, quarter)
        total = rsa[q, 2] + rsb[q, 11] + yr[q // 2, 2, part, :] + pw[slots + 1, qrows(q), :]
        zrow[c, qrows(q), :] = total
        zcol[r, qrows(q), :] = total

    scale = STEP_SIZE / (2.0 * samp)

    def first_half(s):
        factor = scale * ids[2, s].astype(F32)
        grad = dot3(xrow[ids[0, s]], zcol[ids[1, s]], NT)
        tile[s] = tile[s] - factor * grad

    def seen(q, at):
        zh[at, qrows(q), :], zl[at, qrows(q), :] = split(zrow[at, qrows(q), :])

    def own_seen():
        zh[c], zl[c] = split(zrow[c])

    gather_phase(
        zrow, zcol, zrow.at[c], zcol.at[r], zsem, zrsem, own_seen, seen, first_half, 0, lambda: None
    )

    drain(xrow, 15, x_s)
    drain(xcol, 7, xr_s)
    drain(zrow, 15, z_s)
    drain(zcol, 7, zr_s)
    drain(xrow, 15, w_s)
    drain(xcol, 7, y_s)


def finish(tile, zh, zl, xh, xl, ids, out_hbm, diag_hbm, done, out_sem):
    slots = out_hbm.shape[0]
    side, samp = zh.shape[1:]
    scale = STEP_SIZE / (2.0 * samp)
    dot = functools.partial(lax.dot_general, dimension_numbers=NN, preferred_element_type=F32)

    def stepped(s):
        a, b = ids[0, s], ids[1, s]
        za, zb = zh[a], zl[a]
        xa, xb = xh[b], xl[b]
        grad = dot(jnp.concatenate([za, zb, za], 1), jnp.concatenate([xb, xa, xa], 0))
        return tile[s] - scale * ids[2, s].astype(F32) * grad

    def out(s):
        return pltpu.make_async_copy(done.at[s], out_hbm.at[s], out_sem)

    def diag_out():
        return pltpu.make_async_copy(done.at[slots], diag_hbm, out_sem)

    eye = lax.broadcasted_iota(jnp.int32, (side, side), 0) == lax.broadcasted_iota(
        jnp.int32, (side, side), 1
    )
    value = stepped(slots)
    done[slots] = jnp.where(eye, value, shrink(value, STEP_SIZE * PENALTY))
    diag_out().start()

    for s in range(slots):
        done[s] = shrink(stepped(s), STEP_SIZE * PENALTY * ids[2, s].astype(F32))
        out(s).start()

    pltpu.make_async_copy(done, done, out_sem).wait()


def per_device(samples, omega_tiles, omega_diag, tile_rows, tile_cols, tile_active):
    rows, cols = lax.axis_size("row"), lax.axis_size("col")
    samp, side = samples.shape
    slots = omega_tiles.shape[2]
    block = (side, samp)
    dma = pltpu.SemaphoreType.DMA
    vmem = pl.BlockSpec(memory_space=pltpu.VMEM)
    smem = pl.BlockSpec(memory_space=pltpu.SMEM)
    anyw = pl.BlockSpec(memory_space=pl.ANY)
    middle = pl.pallas_call(
        kernel,
        out_shape=(
            pltpu.VMEM((slots + 1, side, side), F32),
            pltpu.VMEM((cols,) + block, BF16),
            pltpu.VMEM((cols,) + block, BF16),
            pltpu.VMEM((rows, samp, side), BF16),
            pltpu.VMEM((rows, samp, side), BF16),
            pltpu.SMEM((3, slots + 1), jnp.int32),
        ),
        in_specs=[anyw] * 6,
        out_specs=(vmem,) * 5 + (smem,),
        scratch_shapes=[
            pltpu.VMEM((samp, side), F32),
            pltpu.VMEM(block, F32),
            pltpu.VMEM((cols,) + block, F32),
            pltpu.VMEM((rows,) + block, F32),
            pltpu.VMEM((cols,) + block, F32),
            pltpu.VMEM((rows,) + block, F32),
            pltpu.VMEM((slots + 2,) + block, F32),
            pltpu.VMEM((slots + 1,) + block, F32),
            pltpu.VMEM((4, 4, side // 4, samp), F32),
            pltpu.VMEM((4, 12, side // 4, samp), F32),
            pltpu.VMEM((4, 3, side // 4, samp), F32),
            pltpu.VMEM((2, 4, side // 2, samp), F32),
            pltpu.VMEM((2, 4, side // 2, samp), F32),
            pltpu.VMEM((2, 3, side // 2, samp), F32),
            pltpu.SMEM((2, 16), jnp.int32),
            pltpu.VMEM((slots,), jnp.int32),
            pltpu.VMEM((slots,), jnp.int32),
            pltpu.VMEM((slots,), jnp.int32),
            pltpu.VMEM((8, 128), jnp.int32),
            pltpu.SMEM((8, 128), jnp.int32),
            dma((4, 3)), dma((4, 8)), dma(()), dma(()), dma((2, 3)), dma((2,)),
            dma((4, 3)), dma((4, 12)), dma((2, 3)), dma((2, 4)),
            dma(()), dma(()), dma(()), dma(()), dma(()), dma(()), dma((7,)),
        ],
        compiler_params=pltpu.CompilerParams(
            collective_id=0, has_side_effects=True, vmem_limit_bytes=48 * 1024 * 1024
        ),
    )(
        samples,
        omega_tiles.reshape(slots, side, side),
        omega_diag,
        tile_rows.reshape(slots),
        tile_cols.reshape(slots),
        tile_active.reshape(slots),
    )
    new_tiles, new_diag = pl.pallas_call(
        finish,
        out_shape=(
            jax.ShapeDtypeStruct((slots, side, side), F32),
            jax.ShapeDtypeStruct((side, side), F32),
        ),
        in_specs=[vmem] * 5 + [smem],
        out_specs=(anyw, anyw),
        scratch_shapes=[pltpu.VMEM((slots + 1, side, side), F32), dma(())],
        compiler_params=pltpu.CompilerParams(vmem_limit_bytes=16 * 1024 * 1024),
    )(*middle)
    return new_tiles[None, None], new_diag


def solution(mesh):
    in_specs = (
        P(None, ("row", "col")),
        P("row", "col", None, None, None),
        P(("row", "col"), None),
        P("row", "col", None),
        P("row", "col", None),
        P("row", "col", None),
    )
    out_specs = (P("row", "col", None, None, None), P(("row", "col"), None))
    return jax.shard_map(
        per_device, mesh=mesh, in_specs=in_specs, out_specs=out_specs, check_vma=False
    )
```

```python
import functools

import jax
import jax.numpy as jnp
from jax import lax
from jax.experimental import pallas as pl
from jax.experimental.pallas import tpu as pltpu
from jax.sharding import PartitionSpec as P

MESH = pl.DeviceIdType.MESH
F32 = jnp.float32
BF16 = jnp.bfloat16
STEP_SIZE = 0.05
PENALTY = 4.0
SIDE = 4
NN = (((1,), (0,)), ((), ()))
NT = (((1,), (1,)), ((), ()))
TN = (((0,), (0,)), ((), ()))
ROUTES = ((True, 1), (True, -1), (False, 1), (False, -1))

ORDER = (
    "xs0", "xs1", "xa00", "xa01", "xb00", "xx00", "xx01", "xa10", "xa11", "xb01", "xb11",
    "xx11", "xa20", "prep", "xb10", "xx10", "xb20", "xa21", "xb30", "xb21", "xb31", "xb40",
    "xx20", "xb50", "xb60", "xb41", "xb51", "xx21", "xh", "wp0", "xb61", "xb71", "wp1", "xb70",
    "wp2", "wp3", "w011", "w000", "w030", "w001", "w031", "w010", "xl", "yp0", "yp1", "w100",
    "w111", "w020", "yp2", "w101", "yp3", "ye00", "w110", "w021", "ye01", "w200", "yc00",
    "ye10", "ye20", "w211", "ye11", "yc01", "split", "w201", "w120", "w210", "yc10", "w300",
    "w121", "yc11", "w311", "yr10", "w131", "ye30", "ye21", "w130", "yr11", "w301", "yc20",
    "ye31", "yc30", "yc21", "w310", "yc31", "w220", "wa10", "yr20", "w221", "wa11", "yr21",
    "w230", "w320", "wa20", "w231", "w321", "wa21", "w330", "wa30", "yr30", "zs0", "yr31",
    "w331", "wa31", "zs1", "za00", "za01", "zb01", "za10", "zx00", "zx01", "za11", "zb00",
    "zb11", "za20", "za21", "zx10", "zx11", "zb10", "zb21", "zb20", "zb30", "zb40", "zb31",
    "zb41", "zx21", "zb51", "zb50", "zx20", "zh", "gp0", "gp1", "zb60", "zb61", "zb71", "gp2",
    "zb70", "gp3", "zl",
)


def split(v):
    high = v.astype(BF16)
    low = (v - high.astype(F32)).astype(BF16)
    return high, low


def dot3(a, b, dims):
    ah, al = split(a)
    bh, bl = split(b)
    dot = functools.partial(lax.dot_general, dimension_numbers=dims, preferred_element_type=F32)
    return dot(ah, bh) + dot(ah, bl) + dot(al, bh)


def mod4(v):
    return lax.rem(v + 2 * SIDE, SIDE)


def shrink(v, limit):
    return jnp.where(v > 0, 1.0, -1.0) * jnp.maximum(jnp.abs(v) - limit, 0.0)


def kernel(
    samples_hbm, tiles_hbm, diag_hbm, left_hbm, right_hbm, active_hbm,
    tile, zh, zl, xh, xl, ids,
    raw, xt, xrow, xcol, zrow, zcol, pw, py, rs0, rsb, rsa, ys, yx, yr, lists, idv0, idv1, idv2, idv, named,
    ga_r, gb_r, xf_r, zf_r, gh_r, gp_r, wa_r, wb_r, yh_r, yp_r,
    x_s, xr_s, z_s, zr_s, w_s, y_s, in_sem,
):
    slots = left_hbm.shape[0]
    samp, side = raw.shape
    quarter, half = side // 4, side // 2
    r = lax.axis_index("row")
    c = lax.axis_index("col")
    x, core = lax.div(r, 2), lax.rem(r, 2)
    yy, zz = lax.div(c, SIDE), lax.rem(c, SIDE)
    other = 1 - core
    partner = 2 * x + other
    pos_a = [zz if first else yy for first, _ in ROUTES]
    pos_b = [yy if first else zz for first, _ in ROUTES]

    def col_of(q, a, b):
        return b * SIDE + a if ROUTES[q][0] else a * SIDE + b

    def qrows(q):
        return pl.ds(q * quarter, quarter)

    def hrows(g):
        return pl.ds(g * half, half)

    def remote(src, dst, send, recv, row, col):
        return pltpu.make_async_remote_copy(
            src_ref=src, dst_ref=dst, send_sem=send, recv_sem=recv,
            device_id=(row, col), device_id_type=MESH,
        )

    def next_a(q):
        return col_of(q, mod4(pos_a[q] + ROUTES[q][1]), pos_b[q])

    def next_b(q):
        return col_of(q, pos_a[q], mod4(pos_b[q] + ROUTES[q][1]))

    def next_x(g):
        return 2 * mod4(x + (1, -1)[g]) + core

    barrier = pltpu.get_barrier_semaphore()
    peers = [(r, next_a(q)) for q in range(4)]
    peers += [(next_x(0), c), (next_x(1), c), (partner, c)]
    for row, col in peers:
        pl.semaphore_signal(barrier, inc=1, device_id=(row, col), device_id_type=MESH)
    loads = [
        pltpu.make_async_copy(samples_hbm, raw, in_sem.at[0]),
        pltpu.make_async_copy(tiles_hbm, tile.at[pl.ds(0, slots)], in_sem.at[1]),
        pltpu.make_async_copy(diag_hbm, tile.at[slots], in_sem.at[2]),
        pltpu.make_async_copy(left_hbm, idv0, in_sem.at[3]),
        pltpu.make_async_copy(right_hbm, idv1, in_sem.at[4]),
        pltpu.make_async_copy(active_hbm, idv2, in_sem.at[5]),
    ]
    for load in loads:
        load.start()
    loads[0].wait()
    own = raw[...].T
    xt[...] = own
    xrow[c] = own
    xcol[r] = own
    pw[0] = jnp.zeros((side, samp), F32)
    py[0] = jnp.zeros((side, samp), F32)
    pl.semaphore_wait(barrier, len(peers))

    def gather_a(panel, q, h, own, sems):
        d = ROUTES[q][1]
        at = col_of(q, mod4(pos_a[q] - d * h), pos_b[q])
        src = own.at[qrows(q)] if h == 0 else panel.at[at, qrows(q)]
        return remote(src, panel.at[at, qrows(q)], sems[0], ga_r.at[q, h], r, next_a(q))

    def gather_a_arrival(panel, q, h, sems):
        d = ROUTES[q][1]
        at = col_of(q, mod4(pos_a[q] - d * (h + 1)), pos_b[q])
        ref = panel.at[at, qrows(q)]
        return remote(ref, ref, sems[0], ga_r.at[q, h], r, next_a(q))

    def gather_b(panel, q, i, own, sems, last=False):
        d = ROUTES[q][1]
        at = col_of(q, mod4(pos_a[q] - d * lax.rem(i, 4)), mod4(pos_b[q] - d * lax.div(i, 4)))
        src = panel.at[at, qrows(q)] if own is None else own.at[qrows(q)]
        recv = sems[1] if last else gb_r.at[q, i]
        return remote(src, panel.at[at, qrows(q)], sems[0], recv, r, next_b(q))

    def arrived_b(q, i):
        d = ROUTES[q][1]
        return col_of(q, mod4(pos_a[q] - d * lax.rem(i, 4)), mod4(pos_b[q] - d * (lax.div(i, 4) + 1)))

    def gather_b_arrival(panel, q, i, sems):
        ref = panel.at[arrived_b(q, i), qrows(q)]
        return remote(ref, ref, sems[0], gb_r.at[q, i], r, next_b(q))

    def gather_last(panel, sems):
        ref = panel.at[pl.ds(0, 4)]
        return remote(ref, ref, sems[0], sems[1], r, next_b(0))

    def ring(panel, g, h, own, sems):
        at = 2 * mod4(x - (1, -1)[g] * h) + core
        src = own.at[hrows(g)] if h == 0 else panel.at[at, hrows(g)]
        return remote(src, panel.at[at, hrows(g)], sems[0], gh_r.at[g, h], next_x(g), c)

    def ring_arrival(panel, g, h, sems):
        at = 2 * mod4(x - (1, -1)[g] * (h + 1)) + core
        ref = panel.at[at, hrows(g)]
        return remote(ref, ref, sems[0], gh_r.at[g, h], next_x(g), c)

    def hand(panel, g, h, own, sems):
        at = 2 * mod4(x - (1, -1)[g] * h) + core
        src = own.at[hrows(g)] if h == 0 else panel.at[at, hrows(g)]
        return remote(src, panel.at[at, hrows(g)], sems[0], sems[1], partner, c)

    def hand_arrivals(panel, sems):
        ref = panel.at[pl.ds(0, 4)]
        return remote(ref, ref, sems[0], sems[1], partner, c)

    def drain(ref, blocks, sem):
        ref = ref.at[pl.ds(0, blocks)]
        remote(ref, ref, sem, in_sem.at[0], partner, c).wait_send()

    def w_sum(col, rows):
        packed = lists[0, col]
        total = pw[packed & 15, rows, :]
        for j in range(1, 4):
            total = total + pw[lax.shift_right_arithmetic(packed, 4 * j) & 15, rows, :]
        return total

    def y_sum(row, rows):
        packed = lists[1, row]
        total = py[packed & 15, rows, :]
        for j in range(1, 8):
            total = total + py[lax.shift_right_arithmetic(packed, 4 * j) & 15, rows, :]
        return total

    xsem, zsem = (x_s, xf_r), (z_s, zf_r)
    xrsem, zrsem = (xr_s, gp_r.at[0]), (zr_s, gp_r.at[1])

    def start_work():
        for load in loads[3:]:
            load.wait()
        for k, ref in enumerate((idv0, idv1, idv2)):
            idv[pl.ds(k, 1), pl.ds(0, slots)] = ref[...].reshape(1, slots)
        move = pltpu.make_async_copy(idv, named, in_sem.at[6])
        move.start()
        move.wait()
        for s in range(slots):
            for k in range(3):
                ids[k, s] = named[k, s]
        ids[0, slots] = c
        ids[1, slots] = r
        ids[2, slots] = 1

        def packs(which, n):
            @pl.loop(0, n)
            def _(a):
                packed = jnp.int32(0)
                for s in range(slots):
                    ident = named[which, s]
                    packed = jnp.where(ident == a, packed * 16 + (s + 1), packed)
                lists[which, a] = packed

        packs(0, 16)
        packs(1, 8)
        for load in loads[1:3]:
            load.wait()

    def w_product(s):
        pw[s + 1] = dot3(tile[s], xcol[ids[1, s]], NN)

    def y_product(s):
        py[s + 1] = dot3(tile[s], xrow[ids[0, s]], TN)

    def scatter_target(q, h, j):
        d = ROUTES[q][1]
        return col_of(q, mod4(pos_a[q] - d * (j + 1)), mod4(pos_b[q] - d * (h + 1)))

    def scatter_b0(q, j):
        return remote(rs0.at[q, j], rsb.at[q, j], w_s, wb_r.at[q, j], r, next_b(q))

    def scatter_b(q, i):
        return remote(rsb.at[q, i], rsb.at[q, i + 4], w_s, wb_r.at[q, i + 4], r, next_b(q))

    def scatter_b_arrival(q, i):
        return remote(rsb.at[q, i], rsb.at[q, i], w_s, wb_r.at[q, i], r, next_b(q))

    def scatter_a(q, h):
        src = rsb.at[q, 8] if h == 0 else rsa.at[q, h - 1]
        return remote(src, rsa.at[q, h], w_s, wa_r.at[q, h], r, next_a(q))

    def scatter_a_arrival(q, h):
        return remote(rsa.at[q, h], rsa.at[q, h], w_s, wa_r.at[q, h], r, next_a(q))

    def y_target(g, h):
        return mod4(x - (1, -1)[g] * (h + 1))

    def y_give(g, h):
        return remote(ys.at[g, h], yx.at[g, h], y_s, yp_r.at[g, h], partner, c)

    def y_ring(g, h):
        src = yx.at[g, 0] if h == 0 else yr.at[g, h - 1]
        return remote(src, yr.at[g, h], y_s, yh_r.at[g, h], next_x(g), c)

    scale = STEP_SIZE / (2.0 * samp)

    def first_half(s):
        factor = scale * ids[2, s].astype(F32)
        grad = dot3(xrow[ids[0, s]], zcol[ids[1, s]], NT)
        tile[s] = tile[s] - factor * grad

    def work(kind, k):
        product = {"w": w_product, "y": y_product, "g": first_half}[kind]
        top = slots - 1 if kind == "y" else slots

        for n in range(4 * k, min(4 * k + 4, top + 1)):
            product(n)

        if kind == "w" and k == 3:
            eye = lax.broadcasted_iota(jnp.int32, (side, side), 0) == lax.broadcasted_iota(
                jnp.int32, (side, side), 1
            )
            diag = tile[slots]
            tile[slots] = diag + jnp.where(eye, STEP_SIZE / jnp.where(eye, diag, 1.0), 0.0)

    def keep(q, at):
        zh[at, qrows(q), :], zl[at, qrows(q), :] = split(zrow[at, qrows(q), :])

    def split_x():
        @pl.loop(0, xh.shape[0])
        def _(b):
            xh[b], xl[b] = split(xcol[b].T)

    def gather_step(p, step, i, g):
        z = p == "z"
        rowp, colp = (zrow, zcol) if z else (xrow, xcol)
        own_row, own_col = (zrow.at[c], zcol.at[r]) if z else (xt, xt)
        csems, rsems = (zsem, zrsem) if z else (xsem, xrsem)
        routes = (2 * g, 2 * g + 1)
        if step == "s":
            if z:
                for q in routes:
                    part = pl.ds((q % 2) * quarter, quarter)
                    total = rsa[q, 2] + rsb[q, 11] + yr[g, 2, part, :] + pw[slots + 1, qrows(q), :]
                    zrow[c, qrows(q), :] = total
                    zcol[r, qrows(q), :] = total
            for q in routes:
                gather_a(rowp, q, 0, own_row, csems).start()
            ring(colp, g, 0, own_col, rsems).start()
            hand(colp, g, 0, own_col, rsems).start()
            for q in routes:
                gather_b(rowp, q, 0, own_row, csems).start()
            if z:
                for q in routes:
                    keep(q, c)
        elif step == "a":
            for q in routes:
                gather_a_arrival(rowp, q, i, csems).wait_recv()
                if i < 2:
                    gather_a(rowp, q, i + 1, own_row, csems).start()
            for q in routes:
                gather_b(rowp, q, i + 1, None, csems).start()
            if z:
                for q in routes:
                    keep(q, col_of(q, mod4(pos_a[q] - ROUTES[q][1] * (i + 1)), pos_b[q]))
        elif step == "b":
            for q in routes:
                gather_b_arrival(rowp, q, i, csems).wait_recv()
                gather_b(rowp, q, i + 4, None, csems, i >= 4).start()
            if z:
                for q in routes:
                    keep(q, arrived_b(q, i))
        elif step == "x":
            ring_arrival(colp, g, i, rsems).wait_recv()
            if i < 2:
                ring(colp, g, i + 1, own_col, rsems).start()
            hand(colp, g, i + 1, own_col, rsems).start()
        elif step == "h":
            hand_arrivals(colp, rsems).wait_recv()
        else:
            gather_last(rowp, csems).wait_recv()
            if z:

                @pl.loop(8, 12)
                def _(n):
                    for q in range(4):
                        keep(q, arrived_b(q, n))

    def scatter_step(h, j, g):
        routes = (2 * g, 2 * g + 1)
        i = (h - 1) * 4 + j
        for q in routes:
            if h == 0:
                rs0[q, j] = w_sum(scatter_target(q, 0, j), qrows(q))
            else:
                scatter_b_arrival(q, i).wait_recv()
                rsb[q, i] = rsb[q, i] + w_sum(scatter_target(q, h, j), qrows(q))
        for q in routes:
            if h == 0:
                scatter_b0(q, j).start()
            elif h < 3:
                scatter_b(q, i).start()
            elif j == 0:
                scatter_a(q, 0).start()

    def scatter_turn(n, g):
        routes = (2 * g, 2 * g + 1)
        for q in routes:
            scatter_a_arrival(q, n - 1).wait_recv()
            if n < 3:
                rsa[q, n - 1] = rsa[q, n - 1] + rsb[q, 8 + n]
        if n < 3:
            for q in routes:
                scatter_a(q, n).start()

    def y_step(step, h, g):
        if step == "e":
            ys[g, h] = y_sum(2 * y_target(g, h) + other, hrows(g))
            y_give(g, h).start()
        elif step == "c":
            y_give(g, h).wait_recv()
            yx[g, h] = yx[g, h] + y_sum(2 * y_target(g, h) + core, hrows(g))
            if h == 0:
                y_ring(g, 0).start()
        else:
            y_ring(g, h - 1).wait_recv()
            yr[g, h - 1] = yr[g, h - 1] + yx[g, h]
            if h < 3:
                y_ring(g, h).start()

    for name in ORDER:
        kind, step = name[0], name[1]
        numbers = [int(n) for n in name[2:] if n.isdigit()]
        if name == "prep":
            start_work()
        elif name == "split":
            split_x()
        elif step == "p":
            work(kind, numbers[0])
        elif kind in "xz":
            i, g = ([0] + numbers)[-2:] if numbers else (0, 0)
            gather_step(kind, step, i, g)
        elif kind == "w" and step == "a":
            scatter_turn(*numbers)
        elif kind == "w":
            scatter_step(int(step), *numbers)
        else:
            y_step(step, *numbers)

    drain(xrow, 15, x_s)
    drain(xcol, 7, xr_s)
    drain(zrow, 15, z_s)
    drain(zcol, 7, zr_s)
    drain(xrow, 15, w_s)
    drain(xcol, 7, y_s)


def finish(tile, zh, zl, xh, xl, ids, out_hbm, diag_hbm, done, out_sem):
    slots = out_hbm.shape[0]
    side, samp = zh.shape[1:]
    scale = STEP_SIZE / (2.0 * samp)
    dot = functools.partial(lax.dot_general, dimension_numbers=NN, preferred_element_type=F32)

    def stepped(s):
        a, b = ids[0, s], ids[1, s]
        za, zb = zh[a], zl[a]
        xa, xb = xh[b], xl[b]
        grad = dot(jnp.concatenate([za, zb, za], 1), jnp.concatenate([xb, xa, xa], 0))
        return tile[s] - scale * ids[2, s].astype(F32) * grad

    def out(s):
        return pltpu.make_async_copy(done.at[s], out_hbm.at[s], out_sem)

    def diag_out():
        return pltpu.make_async_copy(done.at[slots], diag_hbm, out_sem)

    eye = lax.broadcasted_iota(jnp.int32, (side, side), 0) == lax.broadcasted_iota(
        jnp.int32, (side, side), 1
    )
    value = stepped(slots)
    done[slots] = jnp.where(eye, value, shrink(value, STEP_SIZE * PENALTY))
    diag_out().start()

    for s in range(slots):
        done[s] = shrink(stepped(s), STEP_SIZE * PENALTY * ids[2, s].astype(F32))
        out(s).start()

    pltpu.make_async_copy(done, done, out_sem).wait()


def per_device(samples, omega_tiles, omega_diag, tile_rows, tile_cols, tile_active):
    rows, cols = lax.axis_size("row"), lax.axis_size("col")
    samp, side = samples.shape
    slots = omega_tiles.shape[2]
    block = (side, samp)
    dma = pltpu.SemaphoreType.DMA
    vmem = pl.BlockSpec(memory_space=pltpu.VMEM)
    smem = pl.BlockSpec(memory_space=pltpu.SMEM)
    anyw = pl.BlockSpec(memory_space=pl.ANY)
    middle = pl.pallas_call(
        kernel,
        out_shape=(
            pltpu.VMEM((slots + 1, side, side), F32),
            pltpu.VMEM((cols,) + block, BF16),
            pltpu.VMEM((cols,) + block, BF16),
            pltpu.VMEM((rows, samp, side), BF16),
            pltpu.VMEM((rows, samp, side), BF16),
            pltpu.SMEM((3, slots + 1), jnp.int32),
        ),
        in_specs=[anyw] * 6,
        out_specs=(vmem,) * 5 + (smem,),
        scratch_shapes=[
            pltpu.VMEM((samp, side), F32),
            pltpu.VMEM(block, F32),
            pltpu.VMEM((cols,) + block, F32),
            pltpu.VMEM((rows,) + block, F32),
            pltpu.VMEM((cols,) + block, F32),
            pltpu.VMEM((rows,) + block, F32),
            pltpu.VMEM((slots + 2,) + block, F32),
            pltpu.VMEM((slots + 1,) + block, F32),
            pltpu.VMEM((4, 4, side // 4, samp), F32),
            pltpu.VMEM((4, 12, side // 4, samp), F32),
            pltpu.VMEM((4, 3, side // 4, samp), F32),
            pltpu.VMEM((2, 4, side // 2, samp), F32),
            pltpu.VMEM((2, 4, side // 2, samp), F32),
            pltpu.VMEM((2, 3, side // 2, samp), F32),
            pltpu.SMEM((2, 16), jnp.int32),
            pltpu.VMEM((slots,), jnp.int32),
            pltpu.VMEM((slots,), jnp.int32),
            pltpu.VMEM((slots,), jnp.int32),
            pltpu.VMEM((8, 128), jnp.int32),
            pltpu.SMEM((8, 128), jnp.int32),
            dma((4, 3)), dma((4, 8)), dma(()), dma(()), dma((2, 3)), dma((2,)),
            dma((4, 3)), dma((4, 12)), dma((2, 3)), dma((2, 4)),
            dma(()), dma(()), dma(()), dma(()), dma(()), dma(()), dma((7,)),
        ],
        compiler_params=pltpu.CompilerParams(
            collective_id=0, has_side_effects=True, vmem_limit_bytes=48 * 1024 * 1024
        ),
    )(
        samples,
        omega_tiles.reshape(slots, side, side),
        omega_diag,
        tile_rows.reshape(slots),
        tile_cols.reshape(slots),
        tile_active.reshape(slots),
    )
    new_tiles, new_diag = pl.pallas_call(
        finish,
        out_shape=(
            jax.ShapeDtypeStruct((slots, side, side), F32),
            jax.ShapeDtypeStruct((side, side), F32),
        ),
        in_specs=[vmem] * 5 + [smem],
        out_specs=(anyw, anyw),
        scratch_shapes=[pltpu.VMEM((slots + 1, side, side), F32), dma(())],
        compiler_params=pltpu.CompilerParams(vmem_limit_bytes=16 * 1024 * 1024),
    )(*middle)
    return new_tiles[None, None], new_diag


def solution(mesh):
    in_specs = (
        P(None, ("row", "col")),
        P("row", "col", None, None, None),
        P(("row", "col"), None),
        P("row", "col", None),
        P("row", "col", None),
        P("row", "col", None),
    )
    out_specs = (P("row", "col", None, None, None), P(("row", "col"), None))
    return jax.shard_map(
        per_device, mesh=mesh, in_specs=in_specs, out_specs=out_specs, check_vma=False
    )
```

```python
import functools

import jax
import jax.numpy as jnp
from jax import lax
from jax.experimental import pallas as pl
from jax.experimental.pallas import tpu as pltpu
from jax.sharding import PartitionSpec as P

MESH = pl.DeviceIdType.MESH
F32 = jnp.float32
BF16 = jnp.bfloat16
STEP_SIZE = 0.05
PENALTY = 4.0
SIDE = 4
NN = (((1,), (0,)), ((), ()))
NT = (((1,), (1,)), ((), ()))
TN = (((0,), (0,)), ((), ()))
ROUTES = ((True, 1), (True, -1), (False, 1), (False, -1))

ORDER = (
    "xs0", "xs1", "xa00", "xa01", "xx01", "xa10", "xb01", "xx00", "xa11", "xb11", "xb00",
    "prep", "xa20", "xx10", "xa21", "xx11", "xb10", "xb20", "xb21", "xb30", "xb40", "xb31",
    "xx20", "xb41", "xb51", "xb50", "xb60", "xx21", "xh", "xb61", "wp0", "wp1", "wp2", "xb70",
    "wp3", "wp4", "xb71", "wp5", "wp6", "wp7", "w000", "w010", "w001", "w011", "w020", "w031",
    "xl", "yp0", "yp1", "yp2", "yp3", "w100", "w101", "w030", "yp4", "w021", "yp5", "w110",
    "w111", "yp6", "yp7", "ye00", "ye10", "ye01", "yc00", "w200", "yc01", "w201", "w121",
    "w120", "ye20", "yc10", "ye11", "ye21", "ye30", "ye31", "w210", "yc11", "w300", "w301",
    "yr10", "w211", "w220", "yr11", "w221", "w310", "wa10", "yc21", "w130", "yc31", "w311",
    "yc20", "wa11", "w131", "w320", "yr20", "yr21", "w230", "w321", "wa20", "w231", "wa21",
    "yc30", "yr30", "w330", "wa30", "zs0", "yr31", "split", "w331", "wa31", "zs1", "za00",
    "za01", "zx00", "zb01", "za10", "zx01", "za11", "zb11", "zb00", "za20", "zx11", "za21",
    "zx10", "zb10", "zb20", "zb21", "zb30", "zb31", "zx20", "zb41", "zx21", "zb40", "zb51",
    "zb50", "zh", "zb60", "gp0", "zb70", "zb61", "zb71", "gp1", "gp2", "gp3", "gp4", "gp5",
    "gp6", "gp7", "zl",
)


def split(v):
    high = v.astype(BF16)
    low = (v - high.astype(F32)).astype(BF16)
    return high, low


def dot3(a, b, dims):
    ah, al = split(a)
    bh, bl = split(b)
    dot = functools.partial(lax.dot_general, dimension_numbers=dims, preferred_element_type=F32)
    return dot(ah, bh) + dot(ah, bl) + dot(al, bh)


def mod4(v):
    return lax.rem(v + 2 * SIDE, SIDE)


def shrink(v, limit):
    return jnp.where(v > 0, 1.0, -1.0) * jnp.maximum(jnp.abs(v) - limit, 0.0)


def kernel(
    samples_hbm, tiles_hbm, diag_hbm, left_hbm, right_hbm, active_hbm,
    tile, zh, zl, xh, xl, ids,
    raw, xt, xrow, xcol, zrow, zcol, pw, py, rs0, rsb, rsa, ys, yx, yr, lists, idv0, idv1, idv2, idv, named,
    ga_r, gb_r, xf_r, zf_r, gh_r, gp_r, wa_r, wb_r, yh_r, yp_r,
    x_s, xr_s, z_s, zr_s, w_s, y_s, in_sem,
):
    slots = left_hbm.shape[0]
    samp, side = raw.shape
    quarter, half = side // 4, side // 2
    r = lax.axis_index("row")
    c = lax.axis_index("col")
    x, core = lax.div(r, 2), lax.rem(r, 2)
    yy, zz = lax.div(c, SIDE), lax.rem(c, SIDE)
    other = 1 - core
    partner = 2 * x + other
    pos_a = [zz if first else yy for first, _ in ROUTES]
    pos_b = [yy if first else zz for first, _ in ROUTES]

    def col_of(q, a, b):
        return b * SIDE + a if ROUTES[q][0] else a * SIDE + b

    def qrows(q):
        return pl.ds(q * quarter, quarter)

    def hrows(g):
        return pl.ds(g * half, half)

    def remote(src, dst, send, recv, row, col):
        return pltpu.make_async_remote_copy(
            src_ref=src, dst_ref=dst, send_sem=send, recv_sem=recv,
            device_id=(row, col), device_id_type=MESH,
        )

    def next_a(q):
        return col_of(q, mod4(pos_a[q] + ROUTES[q][1]), pos_b[q])

    def next_b(q):
        return col_of(q, pos_a[q], mod4(pos_b[q] + ROUTES[q][1]))

    def next_x(g):
        return 2 * mod4(x + (1, -1)[g]) + core

    barrier = pltpu.get_barrier_semaphore()
    peers = [(r, next_a(q)) for q in range(4)]
    peers += [(next_x(0), c), (next_x(1), c), (partner, c)]
    for row, col in peers:
        pl.semaphore_signal(barrier, inc=1, device_id=(row, col), device_id_type=MESH)
    loads = [
        pltpu.make_async_copy(samples_hbm, raw, in_sem.at[0]),
        pltpu.make_async_copy(tiles_hbm, tile.at[pl.ds(0, slots)], in_sem.at[1]),
        pltpu.make_async_copy(diag_hbm, tile.at[slots], in_sem.at[2]),
        pltpu.make_async_copy(left_hbm, idv0, in_sem.at[3]),
        pltpu.make_async_copy(right_hbm, idv1, in_sem.at[4]),
        pltpu.make_async_copy(active_hbm, idv2, in_sem.at[5]),
    ]
    for load in loads:
        load.start()
    loads[0].wait()
    xt[...] = raw[...].T
    pl.semaphore_wait(barrier, len(peers))

    def gather_a(panel, q, h, own, sems):
        d = ROUTES[q][1]
        at = col_of(q, mod4(pos_a[q] - d * h), pos_b[q])
        src = own.at[qrows(q)] if h == 0 else panel.at[at, qrows(q)]
        return remote(src, panel.at[at, qrows(q)], sems[0], ga_r.at[q, h], r, next_a(q))

    def gather_a_arrival(panel, q, h, sems):
        d = ROUTES[q][1]
        at = col_of(q, mod4(pos_a[q] - d * (h + 1)), pos_b[q])
        ref = panel.at[at, qrows(q)]
        return remote(ref, ref, sems[0], ga_r.at[q, h], r, next_a(q))

    def gather_b(panel, q, i, own, sems, last=False):
        d = ROUTES[q][1]
        at = col_of(q, mod4(pos_a[q] - d * lax.rem(i, 4)), mod4(pos_b[q] - d * lax.div(i, 4)))
        src = panel.at[at, qrows(q)] if own is None else own.at[qrows(q)]
        recv = sems[1] if last else gb_r.at[q, i]
        return remote(src, panel.at[at, qrows(q)], sems[0], recv, r, next_b(q))

    def arrived_b(q, i):
        d = ROUTES[q][1]
        return col_of(q, mod4(pos_a[q] - d * lax.rem(i, 4)), mod4(pos_b[q] - d * (lax.div(i, 4) + 1)))

    def gather_b_arrival(panel, q, i, sems):
        ref = panel.at[arrived_b(q, i), qrows(q)]
        return remote(ref, ref, sems[0], gb_r.at[q, i], r, next_b(q))

    def gather_last(panel, sems):
        ref = panel.at[pl.ds(0, 4)]
        return remote(ref, ref, sems[0], sems[1], r, next_b(0))

    def ring(panel, g, h, own, sems):
        at = 2 * mod4(x - (1, -1)[g] * h) + core
        src = own.at[hrows(g)] if h == 0 else panel.at[at, hrows(g)]
        return remote(src, panel.at[at, hrows(g)], sems[0], gh_r.at[g, h], next_x(g), c)

    def ring_arrival(panel, g, h, sems):
        at = 2 * mod4(x - (1, -1)[g] * (h + 1)) + core
        ref = panel.at[at, hrows(g)]
        return remote(ref, ref, sems[0], gh_r.at[g, h], next_x(g), c)

    def hand(panel, g, h, own, sems):
        at = 2 * mod4(x - (1, -1)[g] * h) + core
        src = own.at[hrows(g)] if h == 0 else panel.at[at, hrows(g)]
        return remote(src, panel.at[at, hrows(g)], sems[0], sems[1], partner, c)

    def hand_arrivals(panel, sems):
        ref = panel.at[pl.ds(0, 4)]
        return remote(ref, ref, sems[0], sems[1], partner, c)

    def drain(ref, blocks, sem):
        ref = ref.at[pl.ds(0, blocks)]
        remote(ref, ref, sem, in_sem.at[0], partner, c).wait_send()

    def w_sum(col, rows):
        packed = lists[0, col]
        total = pw[packed & 15, rows, :]
        for j in range(1, 4):
            total = total + pw[lax.shift_right_arithmetic(packed, 4 * j) & 15, rows, :]
        return total

    def y_sum(row, rows):
        packed = lists[1, row]
        total = py[packed & 15, rows, :]
        for j in range(1, 8):
            total = total + py[lax.shift_right_arithmetic(packed, 4 * j) & 15, rows, :]
        return total

    xsem, zsem = (x_s, xf_r), (z_s, zf_r)
    xrsem, zrsem = (xr_s, gp_r.at[0]), (zr_s, gp_r.at[1])

    def start_work():
        xrow[c] = xt[...]
        xcol[r] = xt[...]
        pw[0] = jnp.zeros((side, samp), F32)
        py[0] = jnp.zeros((side, samp), F32)
        for load in loads[3:]:
            load.wait()
        for k, ref in enumerate((idv0, idv1, idv2)):
            idv[pl.ds(k, 1), pl.ds(0, slots)] = ref[...].reshape(1, slots)
        move = pltpu.make_async_copy(idv, named, in_sem.at[6])
        move.start()
        move.wait()
        for s in range(slots):
            for k in range(3):
                ids[k, s] = named[k, s]
        ids[0, slots] = c
        ids[1, slots] = r
        ids[2, slots] = 1

        def packs(which, n):
            @pl.loop(0, n)
            def _(a):
                packed = jnp.int32(0)
                for s in range(slots):
                    ident = named[which, s]
                    packed = jnp.where(ident == a, packed * 16 + (s + 1), packed)
                lists[which, a] = packed

        packs(0, 16)
        packs(1, 8)
        for load in loads[1:3]:
            load.wait()

    def w_product(s):
        pw[s + 1] = dot3(tile[s], xcol[ids[1, s]], NN)

    def y_product(s):
        py[s + 1] = dot3(tile[s], xrow[ids[0, s]], TN)

    def scatter_target(q, h, j):
        d = ROUTES[q][1]
        return col_of(q, mod4(pos_a[q] - d * (j + 1)), mod4(pos_b[q] - d * (h + 1)))

    def scatter_b0(q, j):
        return remote(rs0.at[q, j], rsb.at[q, j], w_s, wb_r.at[q, j], r, next_b(q))

    def scatter_b(q, i):
        return remote(rsb.at[q, i], rsb.at[q, i + 4], w_s, wb_r.at[q, i + 4], r, next_b(q))

    def scatter_b_arrival(q, i):
        return remote(rsb.at[q, i], rsb.at[q, i], w_s, wb_r.at[q, i], r, next_b(q))

    def scatter_a(q, h):
        src = rsb.at[q, 8] if h == 0 else rsa.at[q, h - 1]
        return remote(src, rsa.at[q, h], w_s, wa_r.at[q, h], r, next_a(q))

    def scatter_a_arrival(q, h):
        return remote(rsa.at[q, h], rsa.at[q, h], w_s, wa_r.at[q, h], r, next_a(q))

    def y_target(g, h):
        return mod4(x - (1, -1)[g] * (h + 1))

    def y_give(g, h):
        return remote(ys.at[g, h], yx.at[g, h], y_s, yp_r.at[g, h], partner, c)

    def y_ring(g, h):
        src = yx.at[g, 0] if h == 0 else yr.at[g, h - 1]
        return remote(src, yr.at[g, h], y_s, yh_r.at[g, h], next_x(g), c)

    scale = STEP_SIZE / (2.0 * samp)

    def first_half(s):
        factor = scale * ids[2, s].astype(F32)
        grad = dot3(xrow[ids[0, s]], zcol[ids[1, s]], NT)
        tile[s] = tile[s] - factor * grad

    def work(kind, k):
        product = {"w": w_product, "y": y_product, "g": first_half}[kind]
        top = slots - 1 if kind == "y" else slots

        for n in range(2 * k, min(2 * k + 2, top + 1)):
            product(n)
        if kind == "w" and 2 * k + 1 >= slots:
            eye = lax.broadcasted_iota(jnp.int32, (side, side), 0) == lax.broadcasted_iota(
                jnp.int32, (side, side), 1
            )
            diag = tile[slots]
            tile[slots] = diag + jnp.where(eye, STEP_SIZE / jnp.where(eye, diag, 1.0), 0.0)

    def keep(q, at):
        zh[at, qrows(q), :], zl[at, qrows(q), :] = split(zrow[at, qrows(q), :])

    def split_x():
        @pl.loop(0, xh.shape[0])
        def _(b):
            xh[b], xl[b] = split(xcol[b].T)

    def gather_step(p, step, i, g):
        z = p == "z"
        rowp, colp = (zrow, zcol) if z else (xrow, xcol)
        own_row, own_col = (zrow.at[c], zcol.at[r]) if z else (xt, xt)
        csems, rsems = (zsem, zrsem) if z else (xsem, xrsem)
        routes = (2 * g, 2 * g + 1)
        if step == "s":
            if z:
                for q in routes:
                    part = pl.ds((q % 2) * quarter, quarter)
                    total = rsa[q, 2] + rsb[q, 11] + yr[g, 2, part, :] + pw[slots + 1, qrows(q), :]
                    zrow[c, qrows(q), :] = total
                    zcol[r, qrows(q), :] = total
            for q in routes:
                gather_a(rowp, q, 0, own_row, csems).start()
            ring(colp, g, 0, own_col, rsems).start()
            hand(colp, g, 0, own_col, rsems).start()
            for q in routes:
                gather_b(rowp, q, 0, own_row, csems).start()
            if z:
                for q in routes:
                    keep(q, c)
        elif step == "a":
            for q in routes:
                gather_a_arrival(rowp, q, i, csems).wait_recv()
                if i < 2:
                    gather_a(rowp, q, i + 1, own_row, csems).start()
            for q in routes:
                gather_b(rowp, q, i + 1, None, csems).start()
            if z:
                for q in routes:
                    keep(q, col_of(q, mod4(pos_a[q] - ROUTES[q][1] * (i + 1)), pos_b[q]))
        elif step == "b":
            for q in routes:
                gather_b_arrival(rowp, q, i, csems).wait_recv()
                gather_b(rowp, q, i + 4, None, csems, i >= 4).start()
            if z:
                for q in routes:
                    keep(q, arrived_b(q, i))
        elif step == "x":
            ring_arrival(colp, g, i, rsems).wait_recv()
            if i < 2:
                ring(colp, g, i + 1, own_col, rsems).start()
            hand(colp, g, i + 1, own_col, rsems).start()
        elif step == "h":
            hand_arrivals(colp, rsems).wait_recv()
        else:
            gather_last(rowp, csems).wait_recv()
            if z:

                @pl.loop(8, 12)
                def _(n):
                    for q in range(4):
                        keep(q, arrived_b(q, n))

    def scatter_step(h, j, g):
        routes = (2 * g, 2 * g + 1)
        i = (h - 1) * 4 + j
        for q in routes:
            if h == 0:
                rs0[q, j] = w_sum(scatter_target(q, 0, j), qrows(q))
            else:
                scatter_b_arrival(q, i).wait_recv()
                rsb[q, i] = rsb[q, i] + w_sum(scatter_target(q, h, j), qrows(q))
        for q in routes:
            if h == 0:
                scatter_b0(q, j).start()
            elif h < 3:
                scatter_b(q, i).start()
            elif j == 0:
                scatter_a(q, 0).start()

    def scatter_turn(n, g):
        routes = (2 * g, 2 * g + 1)
        for q in routes:
            scatter_a_arrival(q, n - 1).wait_recv()
            if n < 3:
                rsa[q, n - 1] = rsa[q, n - 1] + rsb[q, 8 + n]
        if n < 3:
            for q in routes:
                scatter_a(q, n).start()

    def y_step(step, h, g):
        if step == "e":
            ys[g, h] = y_sum(2 * y_target(g, h) + other, hrows(g))
            y_give(g, h).start()
        elif step == "c":
            y_give(g, h).wait_recv()
            yx[g, h] = yx[g, h] + y_sum(2 * y_target(g, h) + core, hrows(g))
            if h == 0:
                y_ring(g, 0).start()
        else:
            y_ring(g, h - 1).wait_recv()
            yr[g, h - 1] = yr[g, h - 1] + yx[g, h]
            if h < 3:
                y_ring(g, h).start()

    for name in ORDER:
        kind, step = name[0], name[1]
        numbers = [int(n) for n in name[2:] if n.isdigit()]
        if name == "prep":
            start_work()
        elif name == "split":
            split_x()
        elif step == "p":
            work(kind, numbers[0])
        elif kind in "xz":
            i, g = ([0] + numbers)[-2:] if numbers else (0, 0)
            gather_step(kind, step, i, g)
        elif kind == "w" and step == "a":
            scatter_turn(*numbers)
        elif kind == "w":
            scatter_step(int(step), *numbers)
        else:
            y_step(step, *numbers)

    drain(xrow, 15, x_s)
    drain(xcol, 7, xr_s)
    drain(zrow, 15, z_s)
    drain(zcol, 7, zr_s)
    drain(xrow, 15, w_s)
    drain(xcol, 7, y_s)


def finish(tile, zh, zl, xh, xl, ids, out_hbm, diag_hbm, done, out_sem):
    slots = out_hbm.shape[0]
    side, samp = zh.shape[1:]
    scale = STEP_SIZE / (2.0 * samp)
    dot = functools.partial(lax.dot_general, dimension_numbers=NN, preferred_element_type=F32)

    def stepped(s):
        a, b = ids[0, s], ids[1, s]
        za, zb = zh[a], zl[a]
        xa, xb = xh[b], xl[b]
        grad = dot(jnp.concatenate([za, zb, za], 1), jnp.concatenate([xb, xa, xa], 0))
        return tile[s] - scale * ids[2, s].astype(F32) * grad

    def out(s):
        return pltpu.make_async_copy(done.at[s], out_hbm.at[s], out_sem)

    def diag_out():
        return pltpu.make_async_copy(done.at[slots], diag_hbm, out_sem)

    eye = lax.broadcasted_iota(jnp.int32, (side, side), 0) == lax.broadcasted_iota(
        jnp.int32, (side, side), 1
    )
    value = stepped(slots)
    done[slots] = jnp.where(eye, value, shrink(value, STEP_SIZE * PENALTY))
    diag_out().start()

    for s in range(slots):
        done[s] = shrink(stepped(s), STEP_SIZE * PENALTY * ids[2, s].astype(F32))
        out(s).start()

    pltpu.make_async_copy(done, done, out_sem).wait()


def per_device(samples, omega_tiles, omega_diag, tile_rows, tile_cols, tile_active):
    rows, cols = lax.axis_size("row"), lax.axis_size("col")
    samp, side = samples.shape
    slots = omega_tiles.shape[2]
    block = (side, samp)
    dma = pltpu.SemaphoreType.DMA
    vmem = pl.BlockSpec(memory_space=pltpu.VMEM)
    smem = pl.BlockSpec(memory_space=pltpu.SMEM)
    anyw = pl.BlockSpec(memory_space=pl.ANY)
    middle = pl.pallas_call(
        kernel,
        out_shape=(
            pltpu.VMEM((slots + 1, side, side), F32),
            pltpu.VMEM((cols,) + block, BF16),
            pltpu.VMEM((cols,) + block, BF16),
            pltpu.VMEM((rows, samp, side), BF16),
            pltpu.VMEM((rows, samp, side), BF16),
            pltpu.SMEM((3, slots + 1), jnp.int32),
        ),
        in_specs=[anyw] * 6,
        out_specs=(vmem,) * 5 + (smem,),
        scratch_shapes=[
            pltpu.VMEM((samp, side), F32),
            pltpu.VMEM(block, F32),
            pltpu.VMEM((cols,) + block, F32),
            pltpu.VMEM((rows,) + block, F32),
            pltpu.VMEM((cols,) + block, F32),
            pltpu.VMEM((rows,) + block, F32),
            pltpu.VMEM((slots + 2,) + block, F32),
            pltpu.VMEM((slots + 1,) + block, F32),
            pltpu.VMEM((4, 4, side // 4, samp), F32),
            pltpu.VMEM((4, 12, side // 4, samp), F32),
            pltpu.VMEM((4, 3, side // 4, samp), F32),
            pltpu.VMEM((2, 4, side // 2, samp), F32),
            pltpu.VMEM((2, 4, side // 2, samp), F32),
            pltpu.VMEM((2, 3, side // 2, samp), F32),
            pltpu.SMEM((2, 16), jnp.int32),
            pltpu.VMEM((slots,), jnp.int32),
            pltpu.VMEM((slots,), jnp.int32),
            pltpu.VMEM((slots,), jnp.int32),
            pltpu.VMEM((8, 128), jnp.int32),
            pltpu.SMEM((8, 128), jnp.int32),
            dma((4, 3)), dma((4, 8)), dma(()), dma(()), dma((2, 3)), dma((2,)),
            dma((4, 3)), dma((4, 12)), dma((2, 3)), dma((2, 4)),
            dma(()), dma(()), dma(()), dma(()), dma(()), dma(()), dma((7,)),
        ],
        compiler_params=pltpu.CompilerParams(
            collective_id=0, has_side_effects=True, vmem_limit_bytes=48 * 1024 * 1024
        ),
    )(
        samples,
        omega_tiles.reshape(slots, side, side),
        omega_diag,
        tile_rows.reshape(slots),
        tile_cols.reshape(slots),
        tile_active.reshape(slots),
    )
    new_tiles, new_diag = pl.pallas_call(
        finish,
        out_shape=(
            jax.ShapeDtypeStruct((slots, side, side), F32),
            jax.ShapeDtypeStruct((side, side), F32),
        ),
        in_specs=[vmem] * 5 + [smem],
        out_specs=(anyw, anyw),
        scratch_shapes=[pltpu.VMEM((slots + 1, side, side), F32), dma(())],
        compiler_params=pltpu.CompilerParams(vmem_limit_bytes=16 * 1024 * 1024),
    )(*middle)
    return new_tiles[None, None], new_diag


def solution(mesh):
    in_specs = (
        P(None, ("row", "col")),
        P("row", "col", None, None, None),
        P(("row", "col"), None),
        P("row", "col", None),
        P("row", "col", None),
        P("row", "col", None),
    )
    out_specs = (P("row", "col", None, None, None), P(("row", "col"), None))
    return jax.shard_map(
        per_device, mesh=mesh, in_specs=in_specs, out_specs=out_specs, check_vma=False
    )
```

```python
import functools

import jax
import jax.numpy as jnp
from jax import lax
from jax.experimental import pallas as pl
from jax.experimental.pallas import tpu as pltpu
from jax.sharding import PartitionSpec as P

MESH = pl.DeviceIdType.MESH
F32 = jnp.float32
BF16 = jnp.bfloat16
STEP_SIZE = 0.05
PENALTY = 4.0
SIDE = 4
NN = (((1,), (0,)), ((), ()))
NT = (((1,), (1,)), ((), ()))
TN = (((0,), (0,)), ((), ()))
ROUTES = ((True, 1), (True, -1), (False, 1), (False, -1))

ORDER = (
    "xs0", "xs1", "xa00", "xa01", "xx01", "xa10", "xb01", "xx00", "xa11", "xb11", "xb00",
    "prep", "xa20", "xx10", "xa21", "xx11", "xb10", "xb20", "xb21", "xb30", "xb40", "xb31",
    "xx20", "xb41", "xb51", "xb50", "xb60", "xx21", "xh", "xb61", "wp0", "wp1", "wp2", "xb70",
    "wp3", "wp4", "xb71", "wp5", "wp6", "wp7", "w000", "w010", "w001", "w011", "w020", "w031",
    "xl", "yp0", "yp1", "yp2", "yp3", "w100", "w101", "w030", "yp4", "w021", "yp5", "w110",
    "w111", "yp6", "yp7", "ye00", "ye10", "ye01", "yc00", "w200", "yc01", "w201", "w121",
    "w120", "ye20", "yc10", "ye11", "ye21", "ye30", "ye31", "w210", "yc11", "w300", "w301",
    "yr10", "w211", "w220", "yr11", "w221", "w310", "wa10", "yc21", "w130", "yc31", "w311",
    "yc20", "wa11", "w131", "w320", "yr20", "yr21", "w230", "w321", "wa20", "w231", "wa21",
    "yc30", "yr30", "w330", "wa30", "zs0", "yr31", "split", "w331", "wa31", "zs1", "za00",
    "za01", "zx00", "zb01", "za10", "zx01", "za11", "zb11", "zb00", "za20", "zx11", "za21",
    "zx10", "zb10", "zb20", "zb21", "zb30", "zb31", "zx20", "zb41", "zx21", "zb40", "zb51",
    "zb50", "zh", "zb60", "gp0", "zb70", "zb61", "zb71", "gp1", "gp2", "gp3", "gp4", "gp5",
    "gp6", "gp7", "zl",
)


def split(v):
    high = v.astype(BF16)
    low = (v - high.astype(F32)).astype(BF16)
    return high, low


def dot3(a, b, dims):
    ah, al = split(a)
    bh, bl = split(b)
    dot = functools.partial(lax.dot_general, dimension_numbers=dims, preferred_element_type=F32)
    ka, kb = dims[0][0][0], dims[0][1][0]
    return dot(jnp.concatenate([ah, al, ah], ka), jnp.concatenate([bl, bh, bh], kb))


def mod4(v):
    return lax.rem(v + 2 * SIDE, SIDE)


def shrink(v, limit):
    return jnp.where(v > 0, 1.0, -1.0) * jnp.maximum(jnp.abs(v) - limit, 0.0)


def kernel(
    samples_hbm, tiles_hbm, diag_hbm, left_hbm, right_hbm, active_hbm,
    tile, zh, zl, xh, xl, ids,
    raw, xt, xrow, xcol, zrow, zcol, pw, py, rs0, rsb, rsa, ys, yx, yr, lists, idv0, idv1, idv2, idv, named,
    ga_r, gb_r, xf_r, zf_r, gh_r, gp_r, wa_r, wb_r, yh_r, yp_r,
    x_s, xr_s, z_s, zr_s, w_s, y_s, in_sem,
):
    slots = left_hbm.shape[0]
    samp, side = raw.shape
    quarter, half = side // 4, side // 2
    r = lax.axis_index("row")
    c = lax.axis_index("col")
    x, core = lax.div(r, 2), lax.rem(r, 2)
    yy, zz = lax.div(c, SIDE), lax.rem(c, SIDE)
    other = 1 - core
    partner = 2 * x + other
    pos_a = [zz if first else yy for first, _ in ROUTES]
    pos_b = [yy if first else zz for first, _ in ROUTES]

    def col_of(q, a, b):
        return b * SIDE + a if ROUTES[q][0] else a * SIDE + b

    def qrows(q):
        return pl.ds(q * quarter, quarter)

    def hrows(g):
        return pl.ds(g * half, half)

    def remote(src, dst, send, recv, row, col):
        return pltpu.make_async_remote_copy(
            src_ref=src, dst_ref=dst, send_sem=send, recv_sem=recv,
            device_id=(row, col), device_id_type=MESH,
        )

    def next_a(q):
        return col_of(q, mod4(pos_a[q] + ROUTES[q][1]), pos_b[q])

    def next_b(q):
        return col_of(q, pos_a[q], mod4(pos_b[q] + ROUTES[q][1]))

    def next_x(g):
        return 2 * mod4(x + (1, -1)[g]) + core

    barrier = pltpu.get_barrier_semaphore()
    peers = [(r, next_a(q)) for q in range(4)]
    peers += [(next_x(0), c), (next_x(1), c), (partner, c)]
    for row, col in peers:
        pl.semaphore_signal(barrier, inc=1, device_id=(row, col), device_id_type=MESH)
    loads = [
        pltpu.make_async_copy(samples_hbm, raw, in_sem.at[0]),
        pltpu.make_async_copy(tiles_hbm, tile.at[pl.ds(0, slots)], in_sem.at[1]),
        pltpu.make_async_copy(diag_hbm, tile.at[slots], in_sem.at[2]),
        pltpu.make_async_copy(left_hbm, idv0, in_sem.at[3]),
        pltpu.make_async_copy(right_hbm, idv1, in_sem.at[4]),
        pltpu.make_async_copy(active_hbm, idv2, in_sem.at[5]),
    ]
    for load in loads:
        load.start()
    loads[0].wait()
    xt[...] = raw[...].T
    pl.semaphore_wait(barrier, len(peers))

    def gather_a(panel, q, h, own, sems):
        d = ROUTES[q][1]
        at = col_of(q, mod4(pos_a[q] - d * h), pos_b[q])
        src = own.at[qrows(q)] if h == 0 else panel.at[at, qrows(q)]
        return remote(src, panel.at[at, qrows(q)], sems[0], ga_r.at[q, h], r, next_a(q))

    def gather_a_arrival(panel, q, h, sems):
        d = ROUTES[q][1]
        at = col_of(q, mod4(pos_a[q] - d * (h + 1)), pos_b[q])
        ref = panel.at[at, qrows(q)]
        return remote(ref, ref, sems[0], ga_r.at[q, h], r, next_a(q))

    def gather_b(panel, q, i, own, sems, last=False):
        d = ROUTES[q][1]
        at = col_of(q, mod4(pos_a[q] - d * lax.rem(i, 4)), mod4(pos_b[q] - d * lax.div(i, 4)))
        src = panel.at[at, qrows(q)] if own is None else own.at[qrows(q)]
        recv = sems[1] if last else gb_r.at[q, i]
        return remote(src, panel.at[at, qrows(q)], sems[0], recv, r, next_b(q))

    def arrived_b(q, i):
        d = ROUTES[q][1]
        return col_of(q, mod4(pos_a[q] - d * lax.rem(i, 4)), mod4(pos_b[q] - d * (lax.div(i, 4) + 1)))

    def gather_b_arrival(panel, q, i, sems):
        ref = panel.at[arrived_b(q, i), qrows(q)]
        return remote(ref, ref, sems[0], gb_r.at[q, i], r, next_b(q))

    def gather_last(panel, sems):
        ref = panel.at[pl.ds(0, 4)]
        return remote(ref, ref, sems[0], sems[1], r, next_b(0))

    def ring(panel, g, h, own, sems):
        at = 2 * mod4(x - (1, -1)[g] * h) + core
        src = own.at[hrows(g)] if h == 0 else panel.at[at, hrows(g)]
        return remote(src, panel.at[at, hrows(g)], sems[0], gh_r.at[g, h], next_x(g), c)

    def ring_arrival(panel, g, h, sems):
        at = 2 * mod4(x - (1, -1)[g] * (h + 1)) + core
        ref = panel.at[at, hrows(g)]
        return remote(ref, ref, sems[0], gh_r.at[g, h], next_x(g), c)

    def hand(panel, g, h, own, sems):
        at = 2 * mod4(x - (1, -1)[g] * h) + core
        src = own.at[hrows(g)] if h == 0 else panel.at[at, hrows(g)]
        return remote(src, panel.at[at, hrows(g)], sems[0], sems[1], partner, c)

    def hand_arrivals(panel, sems):
        ref = panel.at[pl.ds(0, 4)]
        return remote(ref, ref, sems[0], sems[1], partner, c)

    def drain(ref, blocks, sem):
        ref = ref.at[pl.ds(0, blocks)]
        remote(ref, ref, sem, in_sem.at[0], partner, c).wait_send()

    def w_sum(col, rows):
        packed = lists[0, col]
        total = pw[packed & 15, rows, :]
        for j in range(1, 4):
            total = total + pw[lax.shift_right_arithmetic(packed, 4 * j) & 15, rows, :]
        return total

    def y_sum(row, rows):
        packed = lists[1, row]
        total = py[packed & 15, rows, :]
        for j in range(1, 8):
            total = total + py[lax.shift_right_arithmetic(packed, 4 * j) & 15, rows, :]
        return total

    xsem, zsem = (x_s, xf_r), (z_s, zf_r)
    xrsem, zrsem = (xr_s, gp_r.at[0]), (zr_s, gp_r.at[1])

    def start_work():
        xrow[c] = xt[...]
        xcol[r] = xt[...]
        pw[0] = jnp.zeros((side, samp), F32)
        py[0] = jnp.zeros((side, samp), F32)
        for load in loads[3:]:
            load.wait()
        for k, ref in enumerate((idv0, idv1, idv2)):
            idv[pl.ds(k, 1), pl.ds(0, slots)] = ref[...].reshape(1, slots)
        move = pltpu.make_async_copy(idv, named, in_sem.at[6])
        move.start()
        move.wait()
        for s in range(slots):
            for k in range(3):
                ids[k, s] = named[k, s]
        ids[0, slots] = c
        ids[1, slots] = r
        ids[2, slots] = 1

        def packs(which, n):
            @pl.loop(0, n)
            def _(a):
                packed = jnp.int32(0)
                for s in range(slots):
                    ident = named[which, s]
                    packed = jnp.where(ident == a, packed * 16 + (s + 1), packed)
                lists[which, a] = packed

        packs(0, 16)
        packs(1, 8)
        for load in loads[1:3]:
            load.wait()

    def w_product(s):
        pw[s + 1] = dot3(tile[s], xcol[ids[1, s]], NN)

    def y_product(s):
        py[s + 1] = dot3(tile[s], xrow[ids[0, s]], TN)

    def scatter_target(q, h, j):
        d = ROUTES[q][1]
        return col_of(q, mod4(pos_a[q] - d * (j + 1)), mod4(pos_b[q] - d * (h + 1)))

    def scatter_b0(q, j):
        return remote(rs0.at[q, j], rsb.at[q, j], w_s, wb_r.at[q, j], r, next_b(q))

    def scatter_b(q, i):
        return remote(rsb.at[q, i], rsb.at[q, i + 4], w_s, wb_r.at[q, i + 4], r, next_b(q))

    def scatter_b_arrival(q, i):
        return remote(rsb.at[q, i], rsb.at[q, i], w_s, wb_r.at[q, i], r, next_b(q))

    def scatter_a(q, h):
        src = rsb.at[q, 8] if h == 0 else rsa.at[q, h - 1]
        return remote(src, rsa.at[q, h], w_s, wa_r.at[q, h], r, next_a(q))

    def scatter_a_arrival(q, h):
        return remote(rsa.at[q, h], rsa.at[q, h], w_s, wa_r.at[q, h], r, next_a(q))

    def y_target(g, h):
        return mod4(x - (1, -1)[g] * (h + 1))

    def y_give(g, h):
        return remote(ys.at[g, h], yx.at[g, h], y_s, yp_r.at[g, h], partner, c)

    def y_ring(g, h):
        src = yx.at[g, 0] if h == 0 else yr.at[g, h - 1]
        return remote(src, yr.at[g, h], y_s, yh_r.at[g, h], next_x(g), c)

    scale = STEP_SIZE / (2.0 * samp)

    def first_half(s):
        factor = scale * ids[2, s].astype(F32)
        grad = dot3(xrow[ids[0, s]], zcol[ids[1, s]], NT)
        tile[s] = tile[s] - factor * grad

    def work(kind, k):
        product = {"w": w_product, "y": y_product, "g": first_half}[kind]
        top = slots - 1 if kind == "y" else slots

        for n in range(2 * k, min(2 * k + 2, top + 1)):
            product(n)
        if kind == "w" and 2 * k + 1 >= slots:
            eye = lax.broadcasted_iota(jnp.int32, (side, side), 0) == lax.broadcasted_iota(
                jnp.int32, (side, side), 1
            )
            diag = tile[slots]
            tile[slots] = diag + jnp.where(eye, STEP_SIZE / jnp.where(eye, diag, 1.0), 0.0)

    def keep(q, at):
        zh[at, qrows(q), :], zl[at, qrows(q), :] = split(zrow[at, qrows(q), :])

    def split_x():
        @pl.loop(0, xh.shape[0])
        def _(b):
            xh[b], xl[b] = split(xcol[b].T)

    def gather_step(p, step, i, g):
        z = p == "z"
        rowp, colp = (zrow, zcol) if z else (xrow, xcol)
        own_row, own_col = (zrow.at[c], zcol.at[r]) if z else (xt, xt)
        csems, rsems = (zsem, zrsem) if z else (xsem, xrsem)
        routes = (2 * g, 2 * g + 1)
        if step == "s":
            if z:
                for q in routes:
                    part = pl.ds((q % 2) * quarter, quarter)
                    total = rsa[q, 2] + rsb[q, 11] + yr[g, 2, part, :] + pw[slots + 1, qrows(q), :]
                    zrow[c, qrows(q), :] = total
                    zcol[r, qrows(q), :] = total
            for q in routes:
                gather_a(rowp, q, 0, own_row, csems).start()
            ring(colp, g, 0, own_col, rsems).start()
            hand(colp, g, 0, own_col, rsems).start()
            for q in routes:
                gather_b(rowp, q, 0, own_row, csems).start()
            if z:
                for q in routes:
                    keep(q, c)
        elif step == "a":
            for q in routes:
                gather_a_arrival(rowp, q, i, csems).wait_recv()
                if i < 2:
                    gather_a(rowp, q, i + 1, own_row, csems).start()
            for q in routes:
                gather_b(rowp, q, i + 1, None, csems).start()
            if z:
                for q in routes:
                    keep(q, col_of(q, mod4(pos_a[q] - ROUTES[q][1] * (i + 1)), pos_b[q]))
        elif step == "b":
            for q in routes:
                gather_b_arrival(rowp, q, i, csems).wait_recv()
                gather_b(rowp, q, i + 4, None, csems, i >= 4).start()
            if z:
                for q in routes:
                    keep(q, arrived_b(q, i))
        elif step == "x":
            ring_arrival(colp, g, i, rsems).wait_recv()
            if i < 2:
                ring(colp, g, i + 1, own_col, rsems).start()
            hand(colp, g, i + 1, own_col, rsems).start()
        elif step == "h":
            hand_arrivals(colp, rsems).wait_recv()
        else:
            gather_last(rowp, csems).wait_recv()
            if z:

                @pl.loop(8, 12)
                def _(n):
                    for q in range(4):
                        keep(q, arrived_b(q, n))

    def scatter_step(h, j, g):
        routes = (2 * g, 2 * g + 1)
        i = (h - 1) * 4 + j
        for q in routes:
            if h == 0:
                rs0[q, j] = w_sum(scatter_target(q, 0, j), qrows(q))
            else:
                scatter_b_arrival(q, i).wait_recv()
                rsb[q, i] = rsb[q, i] + w_sum(scatter_target(q, h, j), qrows(q))
        for q in routes:
            if h == 0:
                scatter_b0(q, j).start()
            elif h < 3:
                scatter_b(q, i).start()
            elif j == 0:
                scatter_a(q, 0).start()

    def scatter_turn(n, g):
        routes = (2 * g, 2 * g + 1)
        for q in routes:
            scatter_a_arrival(q, n - 1).wait_recv()
            if n < 3:
                rsa[q, n - 1] = rsa[q, n - 1] + rsb[q, 8 + n]
        if n < 3:
            for q in routes:
                scatter_a(q, n).start()

    def y_step(step, h, g):
        if step == "e":
            ys[g, h] = y_sum(2 * y_target(g, h) + other, hrows(g))
            y_give(g, h).start()
        elif step == "c":
            y_give(g, h).wait_recv()
            yx[g, h] = yx[g, h] + y_sum(2 * y_target(g, h) + core, hrows(g))
            if h == 0:
                y_ring(g, 0).start()
        else:
            y_ring(g, h - 1).wait_recv()
            yr[g, h - 1] = yr[g, h - 1] + yx[g, h]
            if h < 3:
                y_ring(g, h).start()

    for name in ORDER:
        kind, step = name[0], name[1]
        numbers = [int(n) for n in name[2:] if n.isdigit()]
        if name == "prep":
            start_work()
        elif name == "split":
            split_x()
        elif step == "p":
            work(kind, numbers[0])
        elif kind in "xz":
            i, g = ([0] + numbers)[-2:] if numbers else (0, 0)
            gather_step(kind, step, i, g)
        elif kind == "w" and step == "a":
            scatter_turn(*numbers)
        elif kind == "w":
            scatter_step(int(step), *numbers)
        else:
            y_step(step, *numbers)

    drain(xrow, 15, x_s)
    drain(xcol, 7, xr_s)
    drain(zrow, 15, z_s)
    drain(zcol, 7, zr_s)
    drain(xrow, 15, w_s)
    drain(xcol, 7, y_s)


def finish(tile, zh, zl, xh, xl, ids, out_hbm, diag_hbm, done, out_sem):
    slots = out_hbm.shape[0]
    side, samp = zh.shape[1:]
    scale = STEP_SIZE / (2.0 * samp)
    dot = functools.partial(lax.dot_general, dimension_numbers=NN, preferred_element_type=F32)

    def stepped(s):
        a, b = ids[0, s], ids[1, s]
        za, zb = zh[a], zl[a]
        xa, xb = xh[b], xl[b]
        grad = dot(jnp.concatenate([za, zb, za], 1), jnp.concatenate([xb, xa, xa], 0))
        return tile[s] - scale * ids[2, s].astype(F32) * grad

    def out(s):
        return pltpu.make_async_copy(done.at[s], out_hbm.at[s], out_sem)

    def diag_out():
        return pltpu.make_async_copy(done.at[slots], diag_hbm, out_sem)

    eye = lax.broadcasted_iota(jnp.int32, (side, side), 0) == lax.broadcasted_iota(
        jnp.int32, (side, side), 1
    )
    value = stepped(slots)
    done[slots] = jnp.where(eye, value, shrink(value, STEP_SIZE * PENALTY))
    diag_out().start()

    for s in range(slots):
        done[s] = shrink(stepped(s), STEP_SIZE * PENALTY * ids[2, s].astype(F32))
        out(s).start()

    pltpu.make_async_copy(done, done, out_sem).wait()


def per_device(samples, omega_tiles, omega_diag, tile_rows, tile_cols, tile_active):
    rows, cols = lax.axis_size("row"), lax.axis_size("col")
    samp, side = samples.shape
    slots = omega_tiles.shape[2]
    block = (side, samp)
    dma = pltpu.SemaphoreType.DMA
    vmem = pl.BlockSpec(memory_space=pltpu.VMEM)
    smem = pl.BlockSpec(memory_space=pltpu.SMEM)
    anyw = pl.BlockSpec(memory_space=pl.ANY)
    middle = pl.pallas_call(
        kernel,
        out_shape=(
            pltpu.VMEM((slots + 1, side, side), F32),
            pltpu.VMEM((cols,) + block, BF16),
            pltpu.VMEM((cols,) + block, BF16),
            pltpu.VMEM((rows, samp, side), BF16),
            pltpu.VMEM((rows, samp, side), BF16),
            pltpu.SMEM((3, slots + 1), jnp.int32),
        ),
        in_specs=[anyw] * 6,
        out_specs=(vmem,) * 5 + (smem,),
        scratch_shapes=[
            pltpu.VMEM((samp, side), F32),
            pltpu.VMEM(block, F32),
            pltpu.VMEM((cols,) + block, F32),
            pltpu.VMEM((rows,) + block, F32),
            pltpu.VMEM((cols,) + block, F32),
            pltpu.VMEM((rows,) + block, F32),
            pltpu.VMEM((slots + 2,) + block, F32),
            pltpu.VMEM((slots + 1,) + block, F32),
            pltpu.VMEM((4, 4, side // 4, samp), F32),
            pltpu.VMEM((4, 12, side // 4, samp), F32),
            pltpu.VMEM((4, 3, side // 4, samp), F32),
            pltpu.VMEM((2, 4, side // 2, samp), F32),
            pltpu.VMEM((2, 4, side // 2, samp), F32),
            pltpu.VMEM((2, 3, side // 2, samp), F32),
            pltpu.SMEM((2, 16), jnp.int32),
            pltpu.VMEM((slots,), jnp.int32),
            pltpu.VMEM((slots,), jnp.int32),
            pltpu.VMEM((slots,), jnp.int32),
            pltpu.VMEM((8, 128), jnp.int32),
            pltpu.SMEM((8, 128), jnp.int32),
            dma((4, 3)), dma((4, 8)), dma(()), dma(()), dma((2, 3)), dma((2,)),
            dma((4, 3)), dma((4, 12)), dma((2, 3)), dma((2, 4)),
            dma(()), dma(()), dma(()), dma(()), dma(()), dma(()), dma((7,)),
        ],
        compiler_params=pltpu.CompilerParams(
            collective_id=0, has_side_effects=True, vmem_limit_bytes=48 * 1024 * 1024
        ),
    )(
        samples,
        omega_tiles.reshape(slots, side, side),
        omega_diag,
        tile_rows.reshape(slots),
        tile_cols.reshape(slots),
        tile_active.reshape(slots),
    )
    new_tiles, new_diag = pl.pallas_call(
        finish,
        out_shape=(
            jax.ShapeDtypeStruct((slots, side, side), F32),
            jax.ShapeDtypeStruct((side, side), F32),
        ),
        in_specs=[vmem] * 5 + [smem],
        out_specs=(anyw, anyw),
        scratch_shapes=[pltpu.VMEM((slots + 1, side, side), F32), dma(())],
        compiler_params=pltpu.CompilerParams(vmem_limit_bytes=16 * 1024 * 1024),
    )(*middle)
    return new_tiles[None, None], new_diag


def solution(mesh):
    in_specs = (
        P(None, ("row", "col")),
        P("row", "col", None, None, None),
        P(("row", "col"), None),
        P("row", "col", None),
        P("row", "col", None),
        P("row", "col", None),
    )
    out_specs = (P("row", "col", None, None, None), P(("row", "col"), None))
    return jax.shard_map(
        per_device, mesh=mesh, in_specs=in_specs, out_specs=out_specs, check_vma=False
    )
```
